512 devices in a mesh: rad: 8 (over x, z_hi), ang: 32 (over z_lo, y), ax: 2 (over core).
Axes of the slice: x: 4, y: 8, z: 8 (z_hi: 2, z_lo: 4; z = z_hi * 4 + z_lo), core: 2. Of those that a mesh axis runs over, the one named last changes fastest.
Arguments:
- start_potential: float32 [128, 1536, 256], P('rad', 'ang', 'ax'), may hold values from -6 to 6
- charge_density: float32 [128, 1536, 256], P('rad', 'ang', 'ax'), may hold values from -12 to 12
- box_anchor: int32 [3, 2048], replicated, may hold values from 0 to 31, as said below
- box_extent: int32 [3, 2048], replicated, may hold values from 1 to 2, as said below
- atom_center: float32 [3, 2048], replicated, as said below
- atom_charge: float32 [2048], replicated, may hold values from 0.5 to 2
- atom_place: int32 [2048], replicated, may hold values from 0 to 2047, each once
Outputs:
- potential: float32 [128, 1536, 256], P('rad', 'ang', 'ax')
- forces: float32 [3, 2048], P(None, ('rad', 'ang', 'ax'))
The draws below stay inside these ranges and needn't reach their ends.
Inputs may be any that keep to these rules, and one draw needn't show every extreme that they name: `box_anchor`: box anchors per dimension lie within that dimension's block count, the radial anchor plus extent never passes the last radial block, and at most 8 atoms share one anchor block. `box_extent`: at most 64 atom boxes cover any one block, and in every draw some block is covered by exactly 64. `atom_center`: each atom's center lies inside its box, in the box's unwrapped cell coordinates.
All inputs are finite; a program needn't handle non-finite values.
Results may differ from the reference program's by a relative error of at most 0.0003.
Values sent between devices are 32-bit elements; how exact they have to be, the bound alone decides.
A program may use at most 64 MiB of HBM per device.

```python
import math
import jax
import jax.numpy as jnp
from jax import lax

CR = 16
CA = 48
CZ = 128
SWEEPS = 3
ATOM_DEV = 4
HOME_MOST = 8
NATOMS = 2048
NR = 128
NA = 1536
NZ = 256
N_RAD = 8
N_ANG = 32
N_AX = 2


def box_layout(key):
    blocks = N_RAD * N_ANG * N_AX
    slots_all = blocks * HOME_MOST
    folded = jax.random.fold_in(key, 4021)
    key_rank, key_wall, key_spot, key_span, key_order = jax.random.split(folded, 5)
    slot_ids = jnp.arange(slots_all, dtype=jnp.int32)
    home_block = slot_ids // HOME_MOST
    home_r = home_block // (N_ANG * N_AX)
    home_a = home_block // N_AX % N_ANG
    home_z = home_block % N_AX
    wall_flags = jax.random.randint(key_wall, (N_RAD,), 0, 2, dtype=jnp.int32)
    cluster_r = jax.random.randint(jax.random.fold_in(key_spot, 1), (), 1, N_RAD, dtype=jnp.int32)
    cluster_a = jax.random.randint(jax.random.fold_in(key_spot, 2), (), 0, N_ANG, dtype=jnp.int32)
    cluster_z = jax.random.randint(jax.random.fold_in(key_spot, 3), (), 0, N_AX, dtype=jnp.int32)
    back_r = cluster_r - home_r
    back_a = jnp.remainder(cluster_a - home_a, N_ANG)
    back_z = jnp.remainder(cluster_z - home_z, N_AX)
    cluster = (back_r >= 0) & (back_r <= 1) & (back_a <= 1) & (back_z <= 1)
    noise_bits = jax.random.randint(key_rank, (slots_all,), 0, 2 ** 17, dtype=jnp.int32)
    ranking = (noise_bits + wall_flags[home_r] * 2 ** 17 + cluster.astype(jnp.int32) * 2 ** 18) * slots_all + slot_ids
    chosen = lax.top_k(ranking, ATOM_DEV * blocks)[1]
    chosen = chosen[jax.random.permutation(key_order, ATOM_DEV * blocks)]
    anchor = jnp.stack([home_r[chosen], home_a[chosen], home_z[chosen]])
    reach_back = jnp.stack([back_r[chosen], back_a[chosen], back_z[chosen]])
    inside = cluster[chosen]
    extent = jax.random.randint(key_span, (3, ATOM_DEV * blocks), 1, 3, dtype=jnp.int32)
    extent = jnp.where(inside[None, :], jnp.maximum(extent, reach_back + 1), extent)
    outermost = anchor[0] == N_RAD - 1
    extent = extent.at[0].set(jnp.where(outermost, 1, extent[0]))
    return (anchor.astype(jnp.int32), extent.astype(jnp.int32))


def draw_box_anchor(key, part):
    return box_layout(key)[0]


def draw_box_extent(key, part):
    return box_layout(key)[1]


def draw_atom_center(key, part):
    anchor, extent = box_layout(key)
    fraction = jax.random.uniform(jax.random.fold_in(key, 77), anchor.shape, jnp.float32, 0.25, 0.75)
    block_cells = jnp.array([CR, CA, CZ], jnp.float32)[:, None]
    return (anchor.astype(jnp.float32) + fraction * extent.astype(jnp.float32)) * block_cells


def block_levels(stream_key, shape, cuts, least, high):
    gain = 1.0
    for dim, blocks in cuts:
        steps = jax.random.uniform(jax.random.fold_in(jax.random.fold_in(stream_key, 6), dim), (blocks,), jnp.float32, least / len(cuts), high / len(cuts))
        gain = gain * jnp.repeat(jnp.exp(steps), shape[dim] // blocks).reshape((-1,) + (1,) * (len(shape) - 1 - dim))
    return gain


def gaussian(rng, shape, deviation, bound, cuts=(), kind=jnp.bfloat16):
    entries = jax.random.normal(rng, shape, jnp.float32) * deviation
    if len(cuts) > 0:
        entries = block_levels(rng, shape, cuts, -0.22, 0.18) * entries
    return jnp.clip(entries, min=-bound, max=bound).astype(kind)


def setup_inputs(seed: int = 0) -> dict:
    seeds = jax.random.split(jax.random.key(seed), 8)
    start_potential = gaussian(seeds[0], (NR, NA, NZ), 1.0, 6.0, ((0, 8), (1, 32), (2, 2)), jnp.float32)
    charge_density = gaussian(seeds[1], (NR, NA, NZ), 2.0, 12.0, ((0, 8), (1, 32), (2, 2)), jnp.float32)
    box_anchor = draw_box_anchor(jax.random.fold_in(seeds[7], 71), 0)
    box_extent = draw_box_extent(jax.random.fold_in(seeds[7], 71), 0)
    atom_center = draw_atom_center(jax.random.fold_in(seeds[7], 71), 0)
    atom_charge = jnp.clip(jnp.exp(jax.random.uniform(seeds[5], (NATOMS,), jnp.float32, math.log(0.5), math.log(2.0))), 0.5, 2.0)
    atom_place = jax.random.permutation(seeds[6], NATOMS).astype(jnp.int32)
    return dict(start_potential=start_potential, charge_density=charge_density, box_anchor=box_anchor, box_extent=box_extent, atom_center=atom_center, atom_charge=atom_charge, atom_place=atom_place)


cheb_low = 0.2
cheb_high = 2.0
highest = lax.Precision.HIGHEST

def sweep_weights(total_sweeps):
    middle = 0.5 * (cheb_high + cheb_low)
    spread = 0.5 * (cheb_high - cheb_low)
    return [1.0 / (middle + spread * math.cos(math.pi * (2 * number + 1) / (2 * total_sweeps))) for number in range(total_sweeps)]

def relax_step(center, radial_up, radial_down, angle_next, angle_prev, axial_next, axial_prev, source, radius, angle_step, weight):
    lower_face = radius - 0.5
    upper_face = radius + 0.5
    angular = 1.0 / (radius * radius * (angle_step * angle_step))
    doubled = 2.0 * center
    applied = (upper_face * (center - radial_up) + lower_face * (center - radial_down)) / radius
    applied = applied + angular * (doubled - angle_next - angle_prev) + (doubled - axial_next - axial_prev)
    diagonal = (upper_face + lower_face) / radius + 2.0 * angular + 2.0
    return center + weight * (source - applied) / diagonal

def gaussian_pair(coords, middle_point, width):
    distance = coords - middle_point
    profile = jnp.exp(-(distance * distance) / (2.0 * width * width))
    return (profile, profile * (-distance / (width * width)))

def take_plane(potential, plane_index):
    inside = (plane_index >= 0) & (plane_index < NR)
    clamped = jnp.clip(plane_index, 0, NR - 1).astype(jnp.int32)
    layer = lax.dynamic_index_in_dim(potential, clamped, 0, keepdims=False)
    return jnp.where(inside, layer, jnp.zeros_like(layer))

def plane_update(potential, source_field, weight, angle_step, plane_index):
    center = take_plane(potential, plane_index)
    radial_up = take_plane(potential, plane_index + 1)
    radial_down = take_plane(potential, plane_index - 1)
    source = take_plane(source_field, plane_index)
    radius = 0.5 * NR + plane_index.astype(jnp.float32) + 0.5
    return relax_step(center, radial_up, radial_down, jnp.roll(center, -1, 0), jnp.roll(center, 1, 0), jnp.roll(center, -1, 1), jnp.roll(center, 1, 1), source, radius, angle_step, weight)

def atom_force(padded, anchor, extent, center_pos, charge, angle_step):
    width_rad = CR / 3.0
    width_ang = CA / 3.0
    width_axial = CZ / 3.0
    amplitude = 1.0 / math.sqrt(width_ang * width_axial / width_rad)
    zero_start = (anchor[2] * 0).astype(jnp.int32)
    slab = lax.dynamic_slice(padded, ((anchor[0] * CR).astype(jnp.int32), (anchor[1] * CA).astype(jnp.int32), zero_start), (2 * CR, 2 * CA, NZ))
    local_rad = jnp.arange(2 * CR, dtype=jnp.int32)
    coord_rad = (anchor[0] * CR + local_rad).astype(jnp.float32)
    rad_profile, rad_slope = gaussian_pair(coord_rad, center_pos[0], width_rad)
    keep_rad = local_rad < extent[0] * CR
    rad_profile = jnp.where(keep_rad, rad_profile, 0.0)
    rad_slope = jnp.where(keep_rad, rad_slope, 0.0)
    radius = 0.5 * NR + coord_rad + 0.5
    local_ang = jnp.arange(2 * CA, dtype=jnp.int32)
    coord_ang = (anchor[1] * CA + local_ang).astype(jnp.float32)
    ang_profile, ang_slope = gaussian_pair(coord_ang, center_pos[1], width_ang)
    keep_ang = local_ang < extent[1] * CA
    ang_profile = jnp.where(keep_ang, ang_profile, 0.0)
    ang_slope = jnp.where(keep_ang, ang_slope, 0.0)
    cells_axial = jnp.arange(NZ, dtype=jnp.int32)
    shifted = jnp.remainder(cells_axial - anchor[2] * CZ, NZ)
    coord_axial = (anchor[2] * CZ + shifted).astype(jnp.float32)
    axial_profile, axial_slope = gaussian_pair(coord_axial, center_pos[2], width_axial)
    keep_axial = shifted < extent[2] * CZ
    axial_profile = jnp.where(keep_axial, axial_profile, 0.0)
    axial_slope = jnp.where(keep_axial, axial_slope, 0.0)
    factors = jnp.stack([axial_profile, axial_slope], axis=1)
    projected = jnp.dot(slab.reshape(4 * CR * CA, NZ), factors, precision=highest, preferred_element_type=jnp.float32).reshape(2 * CR, 2 * CA, 2)
    along_r = jnp.einsum('ij,j->i', projected[:, :, 0], ang_profile, precision=highest)
    along_a = jnp.einsum('ij,j->i', projected[:, :, 0], ang_slope, precision=highest)
    along_z = jnp.einsum('ij,j->i', projected[:, :, 1], ang_profile, precision=highest)
    weight_rad = angle_step * radius
    force_r = jnp.sum(weight_rad * rad_slope * along_r)
    force_a = jnp.sum(rad_profile * along_a)
    force_z = jnp.sum(weight_rad * rad_profile * along_z)
    return jnp.stack([force_r, force_a, force_z]) * (charge * amplitude)

def reference(start_potential, charge_density, box_anchor, box_extent, atom_center, atom_charge, atom_place):
    angle_step = 2.0 * math.pi / NA
    weights = sweep_weights(SWEEPS)
    potential = start_potential
    planes = jnp.arange(NR, dtype=jnp.int32)
    for sweep_index in range(SWEEPS):
        current = potential
        potential = lax.map(lambda plane_index: plane_update(current, charge_density, weights[sweep_index], angle_step, plane_index), planes)
    padded = jnp.concatenate([potential, potential[:, :CA]], axis=1)
    padded = jnp.concatenate([padded, jnp.zeros((CR, NA + CA, NZ), jnp.float32)], axis=0)

    def one_atom(atom_index):
        return atom_force(padded, box_anchor[:, atom_index], box_extent[:, atom_index], atom_center[:, atom_index], atom_charge[atom_index], angle_step)
    by_atom = lax.map(one_atom, jnp.arange(NATOMS, dtype=jnp.int32))
    forces = jnp.zeros((3, NATOMS), jnp.float32).at[:, atom_place].set(by_atom.T)
    return (potential, forces)
```

```python
import functools
import math

import jax
import jax.numpy as jnp
from jax import lax
from jax.experimental import pallas as pl
from jax.experimental.pallas import tpu as pltpu
from jax.sharding import PartitionSpec as P

SWEEPS = 3
GHOST = 3
CR, CA, CZ = 16, 48, 128
N_RAD, N_ANG, N_AX = 8, 32, 2
ROWS = CA + 8
PLANES = CR + 2 * GHOST
SLOTS = 256
ATOMS = 2048
MESH = pl.DeviceIdType.MESH
F32, BF16 = jnp.float32, jnp.bfloat16

cheb_low = 0.2
cheb_high = 2.0


def sweep_weights(total_sweeps):
    middle = 0.5 * (cheb_high + cheb_low)
    spread = 0.5 * (cheb_high - cheb_low)
    return [
        1.0 / (middle + spread * math.cos(math.pi * (2 * number + 1) / (2 * total_sweeps)))
        for number in range(total_sweeps)
    ]


def far_first(count):
    return sorted(range(1, count), key=lambda d: -min(d, count - d))


def plane_peers(r, a, x):
    me_x, z_hi, z_lo, me_y = r // 2, lax.rem(r, 2), a // 8, lax.rem(a, 8)
    order = [(dx, dy) for dx in range(4) for dy in range(8) if dx or dy]
    order.sort(key=lambda d: -(min(d[0], 4 - d[0]) + min(d[1], 8 - d[1])))
    for dx, dy in order:
        tx, ty = lax.rem(me_x + dx, 4), lax.rem(me_y + dy, 8)
        yield dx * 8 + dy, (tx * 2 + z_hi, z_lo * 8 + ty, x), tx * 8 + ty


def column_peers(r, a, x):
    me_x, me_y = r // 2, lax.rem(a, 8)
    me = (lax.rem(r, 2) * 4 + a // 8) * 2 + x
    for d in far_first(16):
        t = lax.rem(me + d, 16)
        tz = t // 2
        yield d, (me_x * 2 + tz // 4, lax.rem(tz, 4) * 8 + me_y, lax.rem(t, 2))


def split2(value):
    high = value.astype(BF16)
    return high, (value - high.astype(F32)).astype(BF16)


def split3(value):
    parts = []
    for _ in range(3):
        part = value.astype(BF16).astype(F32)
        parts.append(part)
        value = value - part
    return parts


def shape_pair(distance, valid, width):
    profile = jnp.where(valid, jnp.exp(-(distance * distance) / (2.0 * width * width)), 0.0)
    return profile, profile * (-distance / (width * width))


def iota(shape, dim):
    return lax.broadcasted_iota(jnp.int32, shape, dim)


def nt(left, right):
    return lax.dot_general(left, right, (((1,), (1,)), ((), ())), preferred_element_type=F32)


def slot_table(r, a, x, anchor_ref, extent_ref, center_ref, charge_ref, place_ref):
    anchor = [anchor_ref[d : d + 1, :] for d in range(3)]
    extent = [extent_ref[d : d + 1, :] for d in range(3)]
    back_r = r - anchor[0]
    back_a = (a - anchor[1]) & (N_ANG - 1)
    back_x = (x - anchor[2]) & (N_AX - 1)
    near = (
        (back_r >= -1) & (back_r <= extent[0]) & (((back_a + 1) & (N_ANG - 1)) <= extent[1] + 1)
    )
    mask = jnp.where(near, 1.0, 0.0)
    chunks = ATOMS // 128
    rows = jnp.concatenate([mask[:, 128 * k : 128 * (k + 1)] for k in range(chunks)], axis=0)
    rows16 = rows.astype(BF16)
    before = jnp.where(iota((128, 128), 0) < iota((128, 128), 1), 1.0, 0.0).astype(BF16)
    above = jnp.where(iota((chunks, chunks), 1) < iota((chunks, chunks), 0), 1.0, 0.0).astype(BF16)
    rank = jnp.dot(rows16, before, preferred_element_type=F32)
    rank = rank + jnp.sum(jnp.dot(above, rows16, preferred_element_type=F32), axis=1, keepdims=True)
    rank = jnp.where(rows > 0.5, rank, -1.0)
    slot = iota((SLOTS, 128), 0).astype(F32)
    pick = jnp.concatenate(
        [
            jnp.where(jnp.broadcast_to(rank[k : k + 1, :], (SLOTS, 128)) == slot, 1.0, 0.0).astype(BF16)
            for k in range(chunks)
        ],
        axis=1,
    )
    data = []
    for d, cells in enumerate((CR, CA, CZ)):
        data += split3(center_ref[d : d + 1, :] - (anchor[d] * cells).astype(F32))
    data += split3(charge_ref[...])
    place = place_ref[...]
    data += [v.astype(F32) for v in (back_r, back_a, back_x, *extent)]
    data.append((((place >> 9) * 8) + ((place >> 3) & 7)).astype(F32))
    data.append(
        (((place >> 8) & 1) * 32 + ((place >> 6) & 3) * 8 + (place & 7)).astype(F32)
    )
    data += [jnp.zeros((1, ATOMS), F32)] * 4
    table = nt(pick, jnp.concatenate(data, axis=0).astype(BF16))
    return table.T


def kernel(
    start_ref,
    source_ref,
    anchor_ref,
    extent_ref,
    center_ref,
    charge_ref,
    place_ref,
    out_ref,
    force_ref,
    va,
    vax,
    vb,
    vbx,
    src,
    coef,
    shape_r,
    ax_in,
    full,
    edge,
    rad_in,
    ang_in,
    corner_in,
    part,
    plane_in,
    mine,
    column_in,
    sems,
):
    r, a, x = lax.axis_index("rad"), lax.axis_index("ang"), lax.axis_index("ax")
    up, down = lax.rem(r + 1, N_RAD), lax.rem(r + N_RAD - 1, N_RAD)
    nxt, prv = lax.rem(a + 1, N_ANG), lax.rem(a + N_ANG - 1, N_ANG)
    plane = list(plane_peers(r, a, x))
    column = list(column_peers(r, a, x))
    around = [(up, a, x), (down, a, x), (r, nxt, x), (r, prv, x)]
    around += [(up, nxt, x), (down, nxt, x), (up, prv, x), (down, prv, x)]

    barrier = pltpu.get_barrier_semaphore()
    targets = [p[1] for p in plane] + [p[1] for p in column] + around
    for target in targets:
        pl.semaphore_signal(barrier, inc=1, device_id=target, device_id_type=MESH)

    for ref in (va, vax, vb, vbx, src):
        ref[...] = jnp.zeros_like(ref)
    va[4 : 4 + CR, 0:CA, :] = start_ref[...]
    src[4 : 4 + CR, 0:CA, :] = source_ref[...]

    step = 2.0 * math.pi / (CA * N_ANG)
    index = r * CR + iota((24, CZ), 0) - 4
    radius = 0.5 * (CR * N_RAD) + index.astype(F32) + 0.5
    inside = (index >= 0) & (index < CR * N_RAD)
    upper, lower = (radius + 0.5) / radius, (radius - 0.5) / radius
    angular = 1.0 / (radius * radius * (step * step))
    inverse = jnp.where(inside, 1.0 / (upper + lower + 2.0 * angular + 2.0), 0.0)
    coef[0] = inverse
    coef[1] = inverse * upper
    coef[2] = inverse * lower
    coef[3] = inverse * angular

    lane = iota((ROWS, CZ), 1)
    first, last = lane == 0, lane == CZ - 1
    buffers = [(va, vax), (vb, vbx)]
    for number, weight in enumerate(sweep_weights(SWEEPS)):
        (own, other), (own_new, other_new) = buffers[number % 2], buffers[1 - number % 2]

        def sweep(p, carry, own=own, other=other, own_new=own_new, other_new=other_new, weight=weight):
            c = [jnp.broadcast_to(coef[k, pl.ds(p, 1), :], (ROWS, CZ)) for k in range(4)]
            v, w = own[p], other[p]
            v_next, v_prev = pltpu.roll(v, CZ - 1, 1), pltpu.roll(v, 1, 1)
            w_next, w_prev = pltpu.roll(w, CZ - 1, 1), pltpu.roll(w, 1, 1)
            for here, there, centre, axial, extra in (
                (own, own_new, v, (jnp.where(last, w_next, v_next), jnp.where(first, w_prev, v_prev)), src),
                (other, other_new, w, (jnp.where(last, v_next, w_next), jnp.where(first, v_prev, w_prev)), None),
            ):
                along = axial[0] + axial[1]
                if extra is not None:
                    along = along + extra[p]
                turn = pltpu.roll(centre, ROWS - 1, 0) + pltpu.roll(centre, 1, 0)
                applied = c[0] * along + c[1] * here[p + 1] + c[2] * here[p - 1] + c[3] * turn
                there[p] = centre + weight * (applied - centre)
            return carry

        reach = number + 1
        lax.fori_loop(4 - reach, 4 + CR + reach, sweep, 0)
    own, other = buffers[SWEEPS % 2]

    table = slot_table(r, a, x, anchor_ref, extent_ref, center_ref, charge_ref, place_ref)

    def entry(k):
        return table[k : k + 1, :]

    centre = [entry(3 * d) + entry(3 * d + 1) + entry(3 * d + 2) for d in range(3)]
    charge = entry(9) + entry(10) + entry(11)
    back, span = [entry(12 + d) for d in range(3)], [entry(15 + d) for d in range(3)]
    width = (CR / 3.0, CA / 3.0, CZ / 3.0)
    amplitude = 1.0 / math.sqrt(width[1] * width[2] / width[0])

    cell = iota((24, SLOTS), 0).astype(F32) - GHOST
    d = cell + back[0] * CR
    profile, slope = shape_pair(d - centre[0], (d >= 0.0) & (d < span[0] * CR), width[0])
    arc = step * (0.5 * (CR * N_RAD) + (r * CR).astype(F32) + cell + 0.5)
    shape_r[0] = arc * slope
    shape_r[1] = profile
    shape_r[2] = arc * profile

    row = iota((ROWS, SLOTS), 0)
    d = jnp.where(row >= CA + 4, row - ROWS, row).astype(F32) + back[1] * CA
    d = jnp.where(d < 0.0, d + CA * N_ANG, d)
    d = jnp.where(d >= CA * N_ANG, d - CA * N_ANG, d)
    ang_profile, ang_slope = shape_pair(d - centre[1], d < span[1] * CA, width[1])

    d = iota((2 * CZ, SLOTS), 0).astype(F32) + back[2] * CZ
    d = jnp.where(d >= CZ * N_AX, d - CZ * N_AX, d)
    ax_profile, ax_slope = shape_pair(d - centre[2], d < span[2] * CZ, width[2])
    ax_high, ax_low = split2(jnp.concatenate([ax_profile, ax_slope], axis=1))

    per = PLANES // 2

    def project(part_index, sums):
        first_plane = part_index * per
        block = jnp.concatenate(
            [
                own[pl.ds(1 + first_plane, per)].reshape(per * ROWS, CZ),
                other[pl.ds(1 + first_plane, per)].reshape(per * ROWS, CZ),
            ],
            axis=1,
        )
        high, low = split2(block)
        projected = jnp.dot(high, ax_high, preferred_element_type=F32)
        projected = projected + jnp.dot(high, ax_low, preferred_element_type=F32)
        projected = projected + jnp.dot(low, ax_high, preferred_element_type=F32)
        sums = list(sums)
        for p in range(per):
            along = [jnp.zeros((8, SLOTS), F32)] * 3
            for t in range(ROWS // 8):
                top = p * ROWS + 8 * t
                plain, sloped = projected[top : top + 8, :SLOTS], projected[top : top + 8, SLOTS:]
                ang_p, ang_s = ang_profile[8 * t : 8 * t + 8], ang_slope[8 * t : 8 * t + 8]
                along = [along[0] + plain * ang_p, along[1] + plain * ang_s, along[2] + sloped * ang_p]
            for k in range(3):
                sums[k] = sums[k] + shape_r[k, pl.ds(first_plane + p, 1), :] * along[k]
        return tuple(sums)

    sums = lax.fori_loop(0, 2, project, tuple(jnp.zeros((8, SLOTS), F32) for _ in range(3)))
    strength = charge * amplitude
    force = [jnp.sum(s, axis=0, keepdims=True) * strength for s in sums]

    target, low = entry(18), entry(19)
    to = jnp.where(iota((32, SLOTS), 0).astype(F32) == target, 1.0, 0.0).astype(BF16)
    here = iota((64, SLOTS), 0).astype(F32) == low
    spread = jnp.concatenate([jnp.where(here, f, 0.0) for f in force] + [jnp.zeros((64, SLOTS), F32)], axis=0)
    placed = jnp.zeros((32, 256), F32)
    for piece in split3(spread):
        placed = placed + nt(to, piece.astype(BF16))
    for k in range(32):
        part[k] = placed[k : k + 1, :]

    pl.semaphore_wait(barrier, len(targets))

    def send(source, landing, number, device):
        copy = pltpu.make_async_remote_copy(
            src_ref=source,
            dst_ref=landing,
            send_sem=sems.at[0, number],
            recv_sem=sems.at[1, number],
            device_id=device,
            device_id_type=MESH,
        )
        copy.start()
        return copy

    def wait(ref, side, number):
        pltpu.make_async_copy(ref, ref, sems.at[side, number]).wait()

    ax_copy = send(other.at[pl.ds(1, PLANES)], ax_in, 0, (r, a, 1 - x))
    for slot, device, place in plane:
        send(part.at[place], plane_in.at[slot - 1], 1, device)

    ax_copy.wait()
    for p in range(PLANES):
        value = own[1 + p] + ax_in[p]
        full[p] = value[0:CA]
        edge[0, p] = value[CA : CA + 4]
        edge[1, p] = value[CA + 4 :]
    lo, hi = pl.ds(0, GHOST), pl.ds(PLANES - GHOST, GHOST)
    copies = [
        send(full.at[hi], rad_in.at[0], 2, around[0]),
        send(full.at[lo], rad_in.at[1], 3, around[1]),
        send(edge.at[0, pl.ds(GHOST, CR)], ang_in.at[0], 4, around[2]),
        send(edge.at[1, pl.ds(GHOST, CR)], ang_in.at[1], 5, around[3]),
        send(edge.at[0, hi], corner_in.at[0], 6, around[4]),
        send(edge.at[0, lo], corner_in.at[1], 7, around[5]),
        send(edge.at[1, hi], corner_in.at[2], 8, around[6]),
        send(edge.at[1, lo], corner_in.at[3], 9, around[7]),
    ]
    out_ref[...] = full[pl.ds(GHOST, CR)]

    wait(plane_in, 1, 1)
    me_place = (r // 2) * 8 + lax.rem(a, 8)
    mine[...] = part[me_place] + jnp.sum(plane_in[...], axis=0)
    for slot, device in column:
        send(mine, column_in.at[slot - 1], 10, device)

    for copy in copies[2:]:
        copy.wait()
    out_ref[:, 0:4, :] = out_ref[:, 0:4, :] + ang_in[0]
    out_ref[:, CA - 4 : CA, :] = out_ref[:, CA - 4 : CA, :] + ang_in[1]
    for k, (planes, rows) in enumerate(
        ((slice(0, 3), slice(0, 4)), (slice(13, 16), slice(0, 4)), (slice(0, 3), slice(44, 48)), (slice(13, 16), slice(44, 48)))
    ):
        out_ref[planes, rows, :] = out_ref[planes, rows, :] + corner_in[k]
    for copy in copies[:2]:
        copy.wait()
    out_ref[0:3] = out_ref[0:3] + rad_in[0]
    out_ref[13:16] = out_ref[13:16] + rad_in[1]

    wait(column_in, 1, 10)
    total = mine[...] + jnp.sum(column_in[...], axis=0)
    me_column = (lax.rem(r, 2) * 4 + a // 8) * 2 + x
    for k in range(3):
        turned = pltpu.roll(jnp.broadcast_to(total, (8, 256)), lax.rem(512 - 64 * k - 4 * me_column, 256), 1)
        force_ref[k : k + 1, :] = turned[0:1, 0:4]
    wait(plane_in, 0, 1)
    wait(column_in, 0, 10)


def shards(start_potential, charge_density, box_anchor, box_extent, atom_center, atom_charge, atom_place):
    whole = pl.BlockSpec(memory_space=pltpu.VMEM)
    grid = (PLANES + 2, ROWS, CZ)
    return pl.pallas_call(
        kernel,
        out_shape=(
            jax.ShapeDtypeStruct((CR, CA, CZ), F32),
            jax.ShapeDtypeStruct((3, 4), F32),
        ),
        in_specs=[whole] * 7,
        out_specs=(whole, whole),
        scratch_shapes=[
            *[pltpu.VMEM(grid, F32)] * 5,
            pltpu.VMEM((4, 24, CZ), F32),
            pltpu.VMEM((3, 24, SLOTS), F32),
            pltpu.VMEM((PLANES, ROWS, CZ), F32),
            pltpu.VMEM((PLANES, CA, CZ), F32),
            pltpu.VMEM((2, PLANES, 4, CZ), F32),
            pltpu.VMEM((2, GHOST, CA, CZ), F32),
            pltpu.VMEM((2, CR, 4, CZ), F32),
            pltpu.VMEM((4, GHOST, 4, CZ), F32),
            pltpu.VMEM((32, 1, 256), F32),
            pltpu.VMEM((31, 1, 256), F32),
            pltpu.VMEM((1, 256), F32),
            pltpu.VMEM((15, 1, 256), F32),
            pltpu.SemaphoreType.DMA((2, 11)),
        ],
        compiler_params=pltpu.CompilerParams(
            collective_id=0, has_side_effects=True, vmem_limit_bytes=40 * 1024 * 1024
        ),
    )(
        start_potential,
        charge_density,
        box_anchor,
        box_extent,
        atom_center,
        atom_charge.reshape(1, ATOMS),
        atom_place.reshape(1, ATOMS),
    )


def solution(mesh):
    placed = (P("rad", "ang", "ax"), P("rad", "ang", "ax"), P(), P(), P(), P(), P())
    return jax.shard_map(
        shards,
        mesh=mesh,
        in_specs=placed,
        out_specs=(P("rad", "ang", "ax"), P(None, ("rad", "ang", "ax"))),
        check_vma=False,
    )
```

```python
import functools
import math

import jax
import jax.numpy as jnp
from jax import lax
from jax.experimental import pallas as pl
from jax.experimental.pallas import tpu as pltpu
from jax.sharding import PartitionSpec as P

SWEEPS = 3
GHOST = 3
CR, CA, CZ = 16, 48, 128
N_RAD, N_ANG, N_AX = 8, 32, 2
ROWS = CA + 8
PLANES = CR + 2 * GHOST
SLOTS = 256
ATOMS = 2048
MESH = pl.DeviceIdType.MESH
F32, BF16 = jnp.float32, jnp.bfloat16

cheb_low = 0.2
cheb_high = 2.0


def sweep_weights(total_sweeps):
    middle = 0.5 * (cheb_high + cheb_low)
    spread = 0.5 * (cheb_high - cheb_low)
    return [
        1.0 / (middle + spread * math.cos(math.pi * (2 * number + 1) / (2 * total_sweeps)))
        for number in range(total_sweeps)
    ]


def far_first(count):
    return sorted(range(1, count), key=lambda d: -min(d, count - d))


def plane_peers(r, a, x):
    me_x, z_hi, z_lo, me_y = r // 2, lax.rem(r, 2), a // 8, lax.rem(a, 8)
    order = [(dx, dy) for dx in range(4) for dy in range(8) if dx or dy]
    order.sort(key=lambda d: -(min(d[0], 4 - d[0]) + min(d[1], 8 - d[1])))
    for dx, dy in order:
        tx, ty = lax.rem(me_x + dx, 4), lax.rem(me_y + dy, 8)
        yield dx * 8 + dy, (tx * 2 + z_hi, z_lo * 8 + ty, x), tx * 8 + ty


def column_peers(r, a, x):
    me_x, me_y = r // 2, lax.rem(a, 8)
    me = (lax.rem(r, 2) * 4 + a // 8) * 2 + x
    for d in far_first(16):
        t = lax.rem(me + d, 16)
        tz = t // 2
        yield d, (me_x * 2 + tz // 4, lax.rem(tz, 4) * 8 + me_y, lax.rem(t, 2))


def split2(value):
    high = value.astype(BF16)
    return high, (value - high.astype(F32)).astype(BF16)


def split3(value):
    parts = []
    for _ in range(3):
        part = value.astype(BF16).astype(F32)
        parts.append(part)
        value = value - part
    return parts


def shape_pair(distance, valid, width):
    profile = jnp.where(valid, jnp.exp(-(distance * distance) / (2.0 * width * width)), 0.0)
    return profile, profile * (-distance / (width * width))


def iota(shape, dim):
    return lax.broadcasted_iota(jnp.int32, shape, dim)


def nt(left, right):
    return lax.dot_general(left, right, (((1,), (1,)), ((), ())), preferred_element_type=F32)


def slot_table(r, a, x, anchor_ref, extent_ref, center_ref, charge_ref, place_ref):
    anchor = [anchor_ref[d : d + 1, :] for d in range(3)]
    extent = [extent_ref[d : d + 1, :] for d in range(3)]
    back_r = r - anchor[0]
    back_a = (a - anchor[1]) & (N_ANG - 1)
    back_x = (x - anchor[2]) & (N_AX - 1)
    near = (
        (back_r >= -1) & (back_r <= extent[0]) & (((back_a + 1) & (N_ANG - 1)) <= extent[1] + 1)
    )
    mask = jnp.where(near, 1.0, 0.0)
    chunks = ATOMS // 128
    rows = jnp.concatenate([mask[:, 128 * k : 128 * (k + 1)] for k in range(chunks)], axis=0)
    rows16 = rows.astype(BF16)
    before = jnp.where(iota((128, 128), 0) < iota((128, 128), 1), 1.0, 0.0).astype(BF16)
    above = jnp.where(iota((chunks, chunks), 1) < iota((chunks, chunks), 0), 1.0, 0.0).astype(BF16)
    rank = jnp.dot(rows16, before, preferred_element_type=F32)
    rank = rank + jnp.sum(jnp.dot(above, rows16, preferred_element_type=F32), axis=1, keepdims=True)
    rank = jnp.where(rows > 0.5, rank, -1.0)
    slot = iota((SLOTS, 128), 0).astype(F32)
    pick = jnp.concatenate(
        [
            jnp.where(jnp.broadcast_to(rank[k : k + 1, :], (SLOTS, 128)) == slot, 1.0, 0.0).astype(BF16)
            for k in range(chunks)
        ],
        axis=1,
    )
    data = []
    for d, cells in enumerate((CR, CA, CZ)):
        data += split3(center_ref[d : d + 1, :] - (anchor[d] * cells).astype(F32))
    data += split3(charge_ref[...])
    place = place_ref[...]
    data += [v.astype(F32) for v in (back_r, back_a, back_x, *extent)]
    data.append((((place >> 9) * 8) + ((place >> 3) & 7)).astype(F32))
    data.append(
        (((place >> 8) & 1) * 32 + ((place >> 6) & 3) * 8 + (place & 7)).astype(F32)
    )
    data += [jnp.zeros((1, ATOMS), F32)] * 4
    table = nt(pick, jnp.concatenate(data, axis=0).astype(BF16))
    return table.T


def kernel(
    start_hbm,
    source_hbm,
    anchor_hbm,
    extent_hbm,
    center_hbm,
    charge_hbm,
    place_hbm,
    out_ref,
    force_ref,
    va,
    vax,
    vb,
    vbx,
    src,
    coef,
    shape_r,
    ax_in,
    full,
    edge,
    rad_in,
    ang_in,
    corner_in,
    part,
    plane_in,
    mine,
    column_in,
    anchor_ref,
    extent_ref,
    center_ref,
    charge_ref,
    place_ref,
    sems,
    in_sems,
):
    cells = (pl.ds(4, CR), pl.ds(0, CA))
    fetch = [
        (start_hbm, va.at[cells]),
        (source_hbm, src.at[cells]),
        (anchor_hbm, anchor_ref),
        (extent_hbm, extent_ref),
        (center_hbm, center_ref),
        (charge_hbm, charge_ref),
        (place_hbm, place_ref),
    ]
    fetch = [pltpu.make_async_copy(*pair, in_sems.at[k]) for k, pair in enumerate(fetch)]
    for copy in fetch:
        copy.start()

    r, a, x = lax.axis_index("rad"), lax.axis_index("ang"), lax.axis_index("ax")
    up, down = lax.rem(r + 1, N_RAD), lax.rem(r + N_RAD - 1, N_RAD)
    nxt, prv = lax.rem(a + 1, N_ANG), lax.rem(a + N_ANG - 1, N_ANG)
    plane = list(plane_peers(r, a, x))
    column = list(column_peers(r, a, x))
    around = [(up, a, x), (down, a, x), (r, nxt, x), (r, prv, x)]
    around += [(up, nxt, x), (down, nxt, x), (up, prv, x), (down, prv, x)]

    barrier = pltpu.get_barrier_semaphore()
    targets = [p[1] for p in plane] + [p[1] for p in column] + around
    for target in targets:
        pl.semaphore_signal(barrier, inc=1, device_id=target, device_id_type=MESH)

    va[4 : 4 + CR, CA:, :] = jnp.zeros((CR, ROWS - CA, CZ), F32)
    src[4 : 4 + CR, CA:, :] = jnp.zeros((CR, ROWS - CA, CZ), F32)
    empty = jnp.zeros((ROWS, CZ), F32)
    for p in (0, 1, 2, 3, 20, 21, 22, 23):
        va[p] = empty
    for p in (0, 1, 22, 23):
        vax[p] = empty
    for p in (1, 2, 21, 22):
        vb[p] = empty
        vbx[p] = empty

    step = 2.0 * math.pi / (CA * N_ANG)
    index = r * CR + iota((24, CZ), 0) - 4
    radius = 0.5 * (CR * N_RAD) + index.astype(F32) + 0.5
    inside = (index >= 0) & (index < CR * N_RAD)
    upper, lower = (radius + 0.5) / radius, (radius - 0.5) / radius
    angular = 1.0 / (radius * radius * (step * step))
    inverse = jnp.where(inside, 1.0 / (upper + lower + 2.0 * angular + 2.0), 0.0)
    coef[0] = inverse
    coef[1] = inverse * upper
    coef[2] = inverse * lower
    coef[3] = inverse * angular

    for copy in fetch:
        copy.wait()

    lane = iota((ROWS, CZ), 1)
    first, last = lane == 0, lane == CZ - 1
    buffers = [(va, vax), (vb, vbx)]
    for number, weight in enumerate(sweep_weights(SWEEPS)):
        (own, other), (own_new, other_new) = buffers[number % 2], buffers[1 - number % 2]
        for p in range(3 - number, 5 + CR + number):
            c = [jnp.broadcast_to(coef[k, p : p + 1, :], (ROWS, CZ)) for k in range(4)]
            v = own[p]
            v_next, v_prev = pltpu.roll(v, CZ - 1, 1), pltpu.roll(v, 1, 1)
            if number == 0:
                along = jnp.where(last, 0.0, v_next) + jnp.where(first, 0.0, v_prev)
                across = jnp.where(last, v_next, 0.0) + jnp.where(first, v_prev, 0.0)
                other_new[p] = weight * (c[0] * across)
            else:
                w = other[p]
                w_next, w_prev = pltpu.roll(w, CZ - 1, 1), pltpu.roll(w, 1, 1)
                along = jnp.where(last, w_next, v_next) + jnp.where(first, w_prev, v_prev)
                across = jnp.where(last, v_next, w_next) + jnp.where(first, v_prev, w_prev)
                turn = pltpu.roll(w, ROWS - 1, 0) + pltpu.roll(w, 1, 0)
                applied = c[0] * across + c[1] * other[p + 1] + c[2] * other[p - 1] + c[3] * turn
                other_new[p] = w + weight * (applied - w)
            if 4 <= p < 4 + CR:
                along = along + src[p]
            turn = pltpu.roll(v, ROWS - 1, 0) + pltpu.roll(v, 1, 0)
            applied = c[0] * along + c[1] * own[p + 1] + c[2] * own[p - 1] + c[3] * turn
            own_new[p] = v + weight * (applied - v)
    own, other = buffers[SWEEPS % 2]

    table = slot_table(r, a, x, anchor_ref, extent_ref, center_ref, charge_ref, place_ref)

    def entry(k):
        return table[k : k + 1, :]

    centre = [entry(3 * d) + entry(3 * d + 1) + entry(3 * d + 2) for d in range(3)]
    charge = entry(9) + entry(10) + entry(11)
    back, span = [entry(12 + d) for d in range(3)], [entry(15 + d) for d in range(3)]
    width = (CR / 3.0, CA / 3.0, CZ / 3.0)
    amplitude = 1.0 / math.sqrt(width[1] * width[2] / width[0])

    cell = iota((24, SLOTS), 0).astype(F32) - GHOST
    d = cell + back[0] * CR
    profile, slope = shape_pair(d - centre[0], (d >= 0.0) & (d < span[0] * CR), width[0])
    arc = step * (0.5 * (CR * N_RAD) + (r * CR).astype(F32) + cell + 0.5)
    shape_r[0] = arc * slope
    shape_r[1] = profile
    shape_r[2] = arc * profile

    row = iota((ROWS, SLOTS), 0)
    d = jnp.where(row >= CA + 4, row - ROWS, row).astype(F32) + back[1] * CA
    d = jnp.where(d < 0.0, d + CA * N_ANG, d)
    d = jnp.where(d >= CA * N_ANG, d - CA * N_ANG, d)
    ang_profile, ang_slope = shape_pair(d - centre[1], d < span[1] * CA, width[1])

    d = iota((2 * CZ, SLOTS), 0).astype(F32) + back[2] * CZ
    d = jnp.where(d >= CZ * N_AX, d - CZ * N_AX, d)
    ax_profile, ax_slope = shape_pair(d - centre[2], d < span[2] * CZ, width[2])
    ax_high, ax_low = split2(jnp.concatenate([ax_profile, ax_slope], axis=1))

    per = PLANES // 2

    def project(part_index, sums):
        first_plane = part_index * per
        block = jnp.concatenate(
            [
                own[pl.ds(1 + first_plane, per)].reshape(per * ROWS, CZ),
                other[pl.ds(1 + first_plane, per)].reshape(per * ROWS, CZ),
            ],
            axis=1,
        )
        high, low = split2(block)
        projected = jnp.dot(high, ax_high, preferred_element_type=F32)
        projected = projected + jnp.dot(high, ax_low, preferred_element_type=F32)
        projected = projected + jnp.dot(low, ax_high, preferred_element_type=F32)
        sums = list(sums)
        for p in range(per):
            along = [jnp.zeros((8, SLOTS), F32)] * 3
            for t in range(ROWS // 8):
                top = p * ROWS + 8 * t
                plain, sloped = projected[top : top + 8, :SLOTS], projected[top : top + 8, SLOTS:]
                ang_p, ang_s = ang_profile[8 * t : 8 * t + 8], ang_slope[8 * t : 8 * t + 8]
                along = [along[0] + plain * ang_p, along[1] + plain * ang_s, along[2] + sloped * ang_p]
            for k in range(3):
                sums[k] = sums[k] + shape_r[k, pl.ds(first_plane + p, 1), :] * along[k]
        return tuple(sums)

    sums = lax.fori_loop(0, 2, project, tuple(jnp.zeros((8, SLOTS), F32) for _ in range(3)))
    strength = charge * amplitude
    force = [jnp.sum(s, axis=0, keepdims=True) * strength for s in sums]

    target, low = entry(18), entry(19)
    to = jnp.where(iota((32, SLOTS), 0).astype(F32) == target, 1.0, 0.0).astype(BF16)
    here = iota((64, SLOTS), 0).astype(F32) == low
    spread = jnp.concatenate([jnp.where(here, f, 0.0) for f in force] + [jnp.zeros((64, SLOTS), F32)], axis=0)
    placed = jnp.zeros((32, 256), F32)
    for piece in split3(spread):
        placed = placed + nt(to, piece.astype(BF16))
    for k in range(32):
        part[k] = placed[k : k + 1, :]

    pl.semaphore_wait(barrier, len(targets))

    def send(source, landing, number, device):
        copy = pltpu.make_async_remote_copy(
            src_ref=source,
            dst_ref=landing,
            send_sem=sems.at[0, number],
            recv_sem=sems.at[1, number],
            device_id=device,
            device_id_type=MESH,
        )
        copy.start()
        return copy

    def wait(ref, side, number):
        pltpu.make_async_copy(ref, ref, sems.at[side, number]).wait()

    ax_copy = send(other.at[pl.ds(1, PLANES)], ax_in, 0, (r, a, 1 - x))
    for slot, device, place in plane:
        send(part.at[place], plane_in.at[slot - 1], 1, device)

    ax_copy.wait()
    for p in range(PLANES):
        value = own[1 + p] + ax_in[p]
        full[p] = value[0:CA]
        edge[0, p] = value[CA : CA + 4]
        edge[1, p] = value[CA + 4 :]
    lo, hi = pl.ds(0, GHOST), pl.ds(PLANES - GHOST, GHOST)
    copies = [
        send(full.at[hi], rad_in.at[0], 2, around[0]),
        send(full.at[lo], rad_in.at[1], 3, around[1]),
        send(edge.at[0, pl.ds(GHOST, CR)], ang_in.at[0], 4, around[2]),
        send(edge.at[1, pl.ds(GHOST, CR)], ang_in.at[1], 5, around[3]),
        send(edge.at[0, hi], corner_in.at[0], 6, around[4]),
        send(edge.at[0, lo], corner_in.at[1], 7, around[5]),
        send(edge.at[1, hi], corner_in.at[2], 8, around[6]),
        send(edge.at[1, lo], corner_in.at[3], 9, around[7]),
    ]
    out_ref[...] = full[pl.ds(GHOST, CR)]

    wait(plane_in, 1, 1)
    me_place = (r // 2) * 8 + lax.rem(a, 8)
    mine[...] = part[me_place] + jnp.sum(plane_in[...], axis=0)
    for slot, device in column:
        send(mine, column_in.at[slot - 1], 10, device)

    for copy in copies[2:]:
        copy.wait()
    out_ref[:, 0:4, :] = out_ref[:, 0:4, :] + ang_in[0]
    out_ref[:, CA - 4 : CA, :] = out_ref[:, CA - 4 : CA, :] + ang_in[1]
    for k, (planes, rows) in enumerate(
        ((slice(0, 3), slice(0, 4)), (slice(13, 16), slice(0, 4)), (slice(0, 3), slice(44, 48)), (slice(13, 16), slice(44, 48)))
    ):
        out_ref[planes, rows, :] = out_ref[planes, rows, :] + corner_in[k]
    for copy in copies[:2]:
        copy.wait()
    out_ref[0:3] = out_ref[0:3] + rad_in[0]
    out_ref[13:16] = out_ref[13:16] + rad_in[1]

    wait(column_in, 1, 10)
    total = mine[...] + jnp.sum(column_in[...], axis=0)
    me_column = (lax.rem(r, 2) * 4 + a // 8) * 2 + x
    for k in range(3):
        turned = pltpu.roll(jnp.broadcast_to(total, (8, 256)), lax.rem(512 - 64 * k - 4 * me_column, 256), 1)
        force_ref[k : k + 1, :] = turned[0:1, 0:4]
    wait(plane_in, 0, 1)
    wait(column_in, 0, 10)


def shards(start_potential, charge_density, box_anchor, box_extent, atom_center, atom_charge, atom_place):
    whole = pl.BlockSpec(memory_space=pltpu.VMEM)
    operands = [start_potential, charge_density, box_anchor, box_extent, atom_center]
    operands += [atom_charge.reshape(1, ATOMS), atom_place.reshape(1, ATOMS)]
    grid = (PLANES + 2, ROWS, CZ)
    return pl.pallas_call(
        kernel,
        out_shape=(
            jax.ShapeDtypeStruct((CR, CA, CZ), F32),
            jax.ShapeDtypeStruct((3, 4), F32),
        ),
        in_specs=[pl.BlockSpec(memory_space=pltpu.HBM)] * 7,
        out_specs=(whole, whole),
        scratch_shapes=[
            *[pltpu.VMEM(grid, F32)] * 5,
            pltpu.VMEM((4, 24, CZ), F32),
            pltpu.VMEM((3, 24, SLOTS), F32),
            pltpu.VMEM((PLANES, ROWS, CZ), F32),
            pltpu.VMEM((PLANES, CA, CZ), F32),
            pltpu.VMEM((2, PLANES, 4, CZ), F32),
            pltpu.VMEM((2, GHOST, CA, CZ), F32),
            pltpu.VMEM((2, CR, 4, CZ), F32),
            pltpu.VMEM((4, GHOST, 4, CZ), F32),
            pltpu.VMEM((32, 1, 256), F32),
            pltpu.VMEM((31, 1, 256), F32),
            pltpu.VMEM((1, 256), F32),
            pltpu.VMEM((15, 1, 256), F32),
            pltpu.VMEM((3, ATOMS), jnp.int32),
            pltpu.VMEM((3, ATOMS), jnp.int32),
            pltpu.VMEM((3, ATOMS), F32),
            pltpu.VMEM((1, ATOMS), F32),
            pltpu.VMEM((1, ATOMS), jnp.int32),
            pltpu.SemaphoreType.DMA((2, 11)),
            pltpu.SemaphoreType.DMA((7,)),
        ],
        compiler_params=pltpu.CompilerParams(
            collective_id=0, has_side_effects=True, vmem_limit_bytes=40 * 1024 * 1024
        ),
    )(*[pltpu.with_memory_space_constraint(v, pltpu.HBM) for v in operands])


def solution(mesh):
    placed = (P("rad", "ang", "ax"), P("rad", "ang", "ax"), P(), P(), P(), P(), P())
    return jax.shard_map(
        shards,
        mesh=mesh,
        in_specs=placed,
        out_specs=(P("rad", "ang", "ax"), P(None, ("rad", "ang", "ax"))),
        check_vma=False,
    )
```

```python
import functools
import math

import jax
import jax.numpy as jnp
from jax import lax
from jax.experimental import pallas as pl
from jax.experimental.pallas import tpu as pltpu
from jax.sharding import PartitionSpec as P

SWEEPS = 3
GHOST = 3
CR, CA, CZ = 16, 48, 128
N_RAD, N_ANG, N_AX = 8, 32, 2
ROWS = CA + 8
PLANES = CR + 2 * GHOST
SLOTS = 256
ATOMS = 2048
MESH = pl.DeviceIdType.MESH
F32, BF16 = jnp.float32, jnp.bfloat16

cheb_low = 0.2
cheb_high = 2.0


def sweep_weights(total_sweeps):
    middle = 0.5 * (cheb_high + cheb_low)
    spread = 0.5 * (cheb_high - cheb_low)
    return [
        1.0 / (middle + spread * math.cos(math.pi * (2 * number + 1) / (2 * total_sweeps)))
        for number in range(total_sweeps)
    ]


def far_first(count):
    return sorted(range(1, count), key=lambda d: -min(d, count - d))


def plane_peers(r, a, x):
    me_x, z_hi, z_lo, me_y = r // 2, lax.rem(r, 2), a // 8, lax.rem(a, 8)
    order = [(dx, dy) for dx in range(4) for dy in range(8) if dx or dy]
    order.sort(key=lambda d: -(min(d[0], 4 - d[0]) + min(d[1], 8 - d[1])))
    for dx, dy in order:
        tx, ty = lax.rem(me_x + dx, 4), lax.rem(me_y + dy, 8)
        yield dx * 8 + dy, (tx * 2 + z_hi, z_lo * 8 + ty, x), tx * 8 + ty


def column_peers(r, a, x):
    me_x, me_y = r // 2, lax.rem(a, 8)
    me = (lax.rem(r, 2) * 4 + a // 8) * 2 + x
    for d in far_first(16):
        t = lax.rem(me + d, 16)
        tz = t // 2
        yield d, (me_x * 2 + tz // 4, lax.rem(tz, 4) * 8 + me_y, lax.rem(t, 2))


def split2(value):
    high = value.astype(BF16)
    return high, (value - high.astype(F32)).astype(BF16)


def split3(value):
    parts = []
    for _ in range(3):
        part = value.astype(BF16).astype(F32)
        parts.append(part)
        value = value - part
    return parts


def shape_pair(distance, valid, width):
    profile = jnp.where(valid, jnp.exp(-(distance * distance) / (2.0 * width * width)), 0.0)
    return profile, profile * (-distance / (width * width))


def iota(shape, dim):
    return lax.broadcasted_iota(jnp.int32, shape, dim)


def nt(left, right):
    return lax.dot_general(left, right, (((1,), (1,)), ((), ())), preferred_element_type=F32)


def slot_table(r, a, x, anchor_ref, extent_ref, center_ref, charge_ref, place_ref):
    anchor = [anchor_ref[d : d + 1, :] for d in range(3)]
    extent = [extent_ref[d : d + 1, :] for d in range(3)]
    back_r = r - anchor[0]
    back_a = (a - anchor[1]) & (N_ANG - 1)
    back_x = (x - anchor[2]) & (N_AX - 1)
    near = (
        (back_r >= -1) & (back_r <= extent[0]) & (((back_a + 1) & (N_ANG - 1)) <= extent[1] + 1)
    )
    mask = jnp.where(near, 1.0, 0.0)
    chunks = ATOMS // 128
    rows = jnp.concatenate([mask[:, 128 * k : 128 * (k + 1)] for k in range(chunks)], axis=0)
    rows16 = rows.astype(BF16)
    before = jnp.where(iota((128, 128), 0) < iota((128, 128), 1), 1.0, 0.0).astype(BF16)
    above = jnp.where(iota((chunks, chunks), 1) < iota((chunks, chunks), 0), 1.0, 0.0).astype(BF16)
    rank = jnp.dot(rows16, before, preferred_element_type=F32)
    rank = rank + jnp.sum(jnp.dot(above, rows16, preferred_element_type=F32), axis=1, keepdims=True)
    rank = jnp.where(rows > 0.5, rank, -1.0)
    slot = iota((SLOTS, 128), 0).astype(F32)
    pick = jnp.concatenate(
        [
            jnp.where(jnp.broadcast_to(rank[k : k + 1, :], (SLOTS, 128)) == slot, 1.0, 0.0).astype(BF16)
            for k in range(chunks)
        ],
        axis=1,
    )
    data = []
    for d, cells in enumerate((CR, CA, CZ)):
        data += split3(center_ref[d : d + 1, :] - (anchor[d] * cells).astype(F32))
    data += split3(charge_ref[...])
    place = place_ref[...]
    data += [v.astype(F32) for v in (back_r, back_a, back_x, *extent)]
    data.append((((place >> 9) * 8) + ((place >> 3) & 7)).astype(F32))
    data.append(
        (((place >> 8) & 1) * 32 + ((place >> 6) & 3) * 8 + (place & 7)).astype(F32)
    )
    data += [jnp.zeros((1, ATOMS), F32)] * 4
    table = nt(pick, jnp.concatenate(data, axis=0).astype(BF16))
    return table.T


def kernel(
    start_hbm,
    source_hbm,
    anchor_hbm,
    extent_hbm,
    center_hbm,
    charge_hbm,
    place_hbm,
    out_ref,
    force_ref,
    va,
    vax,
    vb,
    vbx,
    src,
    coef,
    shape_r,
    ax_in,
    full,
    edge,
    rad_in,
    ang_in,
    corner_in,
    part,
    plane_in,
    mine,
    column_in,
    anchor_ref,
    extent_ref,
    center_ref,
    charge_ref,
    place_ref,
    sems,
    in_sems,
):
    cells = (pl.ds(4, CR), pl.ds(0, CA))
    fetch = [
        (start_hbm, va.at[cells]),
        (source_hbm, src.at[cells]),
        (anchor_hbm, anchor_ref),
        (extent_hbm, extent_ref),
        (center_hbm, center_ref),
        (charge_hbm, charge_ref),
        (place_hbm, place_ref),
    ]
    fetch = [pltpu.make_async_copy(*pair, in_sems.at[k]) for k, pair in enumerate(fetch)]
    for copy in fetch:
        copy.start()

    r, a, x = lax.axis_index("rad"), lax.axis_index("ang"), lax.axis_index("ax")
    up, down = lax.rem(r + 1, N_RAD), lax.rem(r + N_RAD - 1, N_RAD)
    nxt, prv = lax.rem(a + 1, N_ANG), lax.rem(a + N_ANG - 1, N_ANG)
    plane = list(plane_peers(r, a, x))
    column = list(column_peers(r, a, x))
    around = [(up, a, x), (down, a, x), (r, nxt, x), (r, prv, x)]
    around += [(up, nxt, x), (down, nxt, x), (up, prv, x), (down, prv, x)]

    barrier = pltpu.get_barrier_semaphore()
    targets = [p[1] for p in plane] + [p[1] for p in column] + around
    for target in targets:
        pl.semaphore_signal(barrier, inc=1, device_id=target, device_id_type=MESH)

    va[4 : 4 + CR, CA:, :] = jnp.zeros((CR, ROWS - CA, CZ), F32)
    src[4 : 4 + CR, CA:, :] = jnp.zeros((CR, ROWS - CA, CZ), F32)
    empty = jnp.zeros((ROWS, CZ), F32)
    for p in (0, 1, 2, 3, 20, 21, 22, 23):
        va[p] = empty
    for p in (0, 1, 22, 23):
        vax[p] = empty
    for p in (1, 2, 21, 22):
        vb[p] = empty
        vbx[p] = empty

    step = 2.0 * math.pi / (CA * N_ANG)
    index = r * CR + iota((24, CZ), 0) - 4
    radius = 0.5 * (CR * N_RAD) + index.astype(F32) + 0.5
    inside = (index >= 0) & (index < CR * N_RAD)
    upper, lower = (radius + 0.5) / radius, (radius - 0.5) / radius
    angular = 1.0 / (radius * radius * (step * step))
    inverse = jnp.where(inside, 1.0 / (upper + lower + 2.0 * angular + 2.0), 0.0)
    coef[0] = inverse
    coef[1] = inverse * upper
    coef[2] = inverse * lower
    coef[3] = inverse * angular

    for copy in fetch:
        copy.wait()

    lane = iota((ROWS, CZ), 1)
    first, last = lane == 0, lane == CZ - 1
    buffers = [(va, vax), (vb, vbx)]
    for number, weight in enumerate(sweep_weights(SWEEPS)):
        (own, other), (own_new, other_new) = buffers[number % 2], buffers[1 - number % 2]
        for p in range(3 - number, 5 + CR + number):
            c = [jnp.broadcast_to(coef[k, p : p + 1, :], (ROWS, CZ)) for k in range(4)]
            v = own[p]
            v_next, v_prev = pltpu.roll(v, CZ - 1, 1), pltpu.roll(v, 1, 1)
            if number == 0:
                along = jnp.where(last, 0.0, v_next) + jnp.where(first, 0.0, v_prev)
                across = jnp.where(last, v_next, 0.0) + jnp.where(first, v_prev, 0.0)
                other_new[p] = weight * (c[0] * across)
            else:
                w = other[p]
                w_next, w_prev = pltpu.roll(w, CZ - 1, 1), pltpu.roll(w, 1, 1)
                along = jnp.where(last, w_next, v_next) + jnp.where(first, w_prev, v_prev)
                across = jnp.where(last, v_next, w_next) + jnp.where(first, v_prev, w_prev)
                turn = pltpu.roll(w, ROWS - 1, 0) + pltpu.roll(w, 1, 0)
                applied = c[0] * across + c[1] * other[p + 1] + c[2] * other[p - 1] + c[3] * turn
                other_new[p] = w + weight * (applied - w)
            if 4 <= p < 4 + CR:
                along = along + src[p]
            turn = pltpu.roll(v, ROWS - 1, 0) + pltpu.roll(v, 1, 0)
            applied = c[0] * along + c[1] * own[p + 1] + c[2] * own[p - 1] + c[3] * turn
            own_new[p] = v + weight * (applied - v)
    own, other = buffers[SWEEPS % 2]

    table = slot_table(r, a, x, anchor_ref, extent_ref, center_ref, charge_ref, place_ref)

    def entry(k):
        return table[k : k + 1, :]

    centre = [entry(3 * d) + entry(3 * d + 1) + entry(3 * d + 2) for d in range(3)]
    charge = entry(9) + entry(10) + entry(11)
    back, span = [entry(12 + d) for d in range(3)], [entry(15 + d) for d in range(3)]
    width = (CR / 3.0, CA / 3.0, CZ / 3.0)
    amplitude = 1.0 / math.sqrt(width[1] * width[2] / width[0])

    cell = iota((24, SLOTS), 0).astype(F32) - GHOST
    d = cell + back[0] * CR
    profile, slope = shape_pair(d - centre[0], (d >= 0.0) & (d < span[0] * CR), width[0])
    arc = step * (0.5 * (CR * N_RAD) + (r * CR).astype(F32) + cell + 0.5)
    shape_r[0] = arc * slope
    shape_r[1] = profile
    shape_r[2] = arc * profile

    row = iota((ROWS, SLOTS), 0)
    d = jnp.where(row >= CA + 4, row - ROWS, row).astype(F32) + back[1] * CA
    d = jnp.where(d < 0.0, d + CA * N_ANG, d)
    d = jnp.where(d >= CA * N_ANG, d - CA * N_ANG, d)
    ang_profile, ang_slope = shape_pair(d - centre[1], d < span[1] * CA, width[1])

    d = iota((2 * CZ, SLOTS), 0).astype(F32) + back[2] * CZ
    d = jnp.where(d >= CZ * N_AX, d - CZ * N_AX, d)
    ax_profile, ax_slope = shape_pair(d - centre[2], d < span[2] * CZ, width[2])
    ax_high, ax_low = split2(jnp.concatenate([ax_profile, ax_slope], axis=1))

    per = PLANES // 2

    def project(part_index, sums):
        first_plane = part_index * per
        block = jnp.concatenate(
            [
                own[pl.ds(1 + first_plane, per)].reshape(per * ROWS, CZ),
                other[pl.ds(1 + first_plane, per)].reshape(per * ROWS, CZ),
            ],
            axis=1,
        )
        high, low = split2(block)
        projected = jnp.dot(high, ax_high, preferred_element_type=F32)
        projected = projected + jnp.dot(high, ax_low, preferred_element_type=F32)
        projected = projected + jnp.dot(low, ax_high, preferred_element_type=F32)
        sums = list(sums)
        for p in range(per):
            along = [jnp.zeros((8, SLOTS), F32)] * 3
            for t in range(ROWS // 8):
                top = p * ROWS + 8 * t
                plain, sloped = projected[top : top + 8, :SLOTS], projected[top : top + 8, SLOTS:]
                ang_p, ang_s = ang_profile[8 * t : 8 * t + 8], ang_slope[8 * t : 8 * t + 8]
                along = [along[0] + plain * ang_p, along[1] + plain * ang_s, along[2] + sloped * ang_p]
            for k in range(3):
                sums[k] = sums[k] + shape_r[k, pl.ds(first_plane + p, 1), :] * along[k]
        return tuple(sums)

    sums = lax.fori_loop(0, 2, project, tuple(jnp.zeros((8, SLOTS), F32) for _ in range(3)))
    strength = charge * amplitude
    force = [jnp.sum(s, axis=0, keepdims=True) * strength for s in sums]

    target, low = entry(18), entry(19)
    to = jnp.where(iota((32, SLOTS), 0).astype(F32) == target, 1.0, 0.0).astype(BF16)
    here = iota((64, SLOTS), 0).astype(F32) == low
    spread = jnp.concatenate([jnp.where(here, f, 0.0) for f in force] + [jnp.zeros((64, SLOTS), F32)], axis=0)
    placed = jnp.zeros((32, 256), F32)
    for piece in split3(spread):
        placed = placed + nt(to, piece.astype(BF16))
    for k in range(32):
        part[k] = placed[k : k + 1, :]

    pl.semaphore_wait(barrier, len(targets))

    def send(source, landing, number, device):
        copy = pltpu.make_async_remote_copy(
            src_ref=source,
            dst_ref=landing,
            send_sem=sems.at[0, number],
            recv_sem=sems.at[1, number],
            device_id=device,
            device_id_type=MESH,
        )
        copy.start()
        return copy

    def wait(ref, side, number):
        pltpu.make_async_copy(ref, ref, sems.at[side, number]).wait()

    for slot, device, place in plane:
        send(part.at[place], plane_in.at[slot - 1], 1, device)
    rows = pl.ds(0, CA)
    far = [
        send(own.at[22, rows], rad_in.at[0, 2], 2, around[0]),
        send(own.at[1, rows], rad_in.at[1, 0], 3, around[1]),
    ]
    partner = (r, a, 1 - x)
    below, above, inner = pl.ds(2, 2), pl.ds(20, 2), pl.ds(4, CR)
    ax_copies = [
        send(other.at[planes], ax_in.at[planes], number, partner)
        for planes, number in ((above, 0), (below, 11), (inner, 12))
    ]

    def join(p):
        value = own[p] + ax_in[p]
        full[p] = value[0:CA]
        edge[0, p] = value[CA : CA + 4]
        edge[1, p] = value[CA + 4 :]

    ax_copies[0].wait_recv()
    join(20)
    join(21)
    near = [send(full.at[above], rad_in.at[0, pl.ds(0, 2)], 13, around[0])]
    ax_copies[1].wait_recv()
    join(2)
    join(3)
    near.append(send(full.at[below], rad_in.at[1, pl.ds(1, 2)], 14, around[1]))
    copies = [
        send(edge.at[0, above], corner_in.at[0], 6, around[4]),
        send(edge.at[0, below], corner_in.at[1], 7, around[5]),
        send(edge.at[1, above], corner_in.at[2], 8, around[6]),
        send(edge.at[1, below], corner_in.at[3], 9, around[7]),
    ]
    ax_copies[2].wait_recv()
    for p in range(4, 4 + CR):
        join(p)
    copies.append(send(edge.at[0, inner], ang_in.at[0], 4, around[2]))
    copies.append(send(edge.at[1, inner], ang_in.at[1], 5, around[3]))
    out_ref[...] = full[inner]

    wait(plane_in, 1, 1)
    me_place = (r // 2) * 8 + lax.rem(a, 8)
    mine[...] = part[me_place] + jnp.sum(plane_in[...], axis=0)
    for slot, device in column:
        send(mine, column_in.at[slot - 1], 10, device)

    for copy in copies:
        copy.wait()
    out_ref[:, 0:4, :] = out_ref[:, 0:4, :] + ang_in[0]
    out_ref[:, CA - 4 : CA, :] = out_ref[:, CA - 4 : CA, :] + ang_in[1]
    for k in range(4):
        planes = pl.ds(14 * (k % 2), 2)
        rows = pl.ds((CA - 4) * (k // 2), 4)
        out_ref[planes, rows, :] = out_ref[planes, rows, :] + corner_in[k]
    for copy in far + near:
        copy.wait()
    out_ref[0:3] = out_ref[0:3] + rad_in[0]
    out_ref[13:16] = out_ref[13:16] + rad_in[1]
    for copy in ax_copies:
        copy.wait_send()

    wait(column_in, 1, 10)
    total = mine[...] + jnp.sum(column_in[...], axis=0)
    me_column = (lax.rem(r, 2) * 4 + a // 8) * 2 + x
    for k in range(3):
        turned = pltpu.roll(jnp.broadcast_to(total, (8, 256)), lax.rem(512 - 64 * k - 4 * me_column, 256), 1)
        force_ref[k : k + 1, :] = turned[0:1, 0:4]
    wait(plane_in, 0, 1)
    wait(column_in, 0, 10)


def store(potential_ref, force_ref, potential_out, force_out, sems):
    copies = [
        pltpu.make_async_copy(potential_ref, potential_out, sems.at[0]),
        pltpu.make_async_copy(force_ref, force_out, sems.at[1]),
    ]
    for copy in copies:
        copy.start()
    for copy in copies:
        copy.wait()


def shards(start_potential, charge_density, box_anchor, box_extent, atom_center, atom_charge, atom_place):
    whole = pl.BlockSpec(memory_space=pltpu.VMEM)
    operands = [start_potential, charge_density, box_anchor, box_extent, atom_center]
    operands += [atom_charge.reshape(1, ATOMS), atom_place.reshape(1, ATOMS)]
    grid = (PLANES + 2, ROWS, CZ)
    potential, forces = pl.pallas_call(
        kernel,
        out_shape=(
            jax.ShapeDtypeStruct((CR, CA, CZ), F32),
            jax.ShapeDtypeStruct((3, 4), F32),
        ),
        in_specs=[pl.BlockSpec(memory_space=pltpu.HBM)] * 7,
        out_specs=(whole, whole),
        scratch_shapes=[
            *[pltpu.VMEM(grid, F32)] * 5,
            pltpu.VMEM((4, 24, CZ), F32),
            pltpu.VMEM((3, 24, SLOTS), F32),
            pltpu.VMEM(grid, F32),
            pltpu.VMEM((PLANES + 2, CA, CZ), F32),
            pltpu.VMEM((2, PLANES + 2, 4, CZ), F32),
            pltpu.VMEM((2, GHOST, CA, CZ), F32),
            pltpu.VMEM((2, CR, 4, CZ), F32),
            pltpu.VMEM((4, 2, 4, CZ), F32),
            pltpu.VMEM((32, 1, 256), F32),
            pltpu.VMEM((31, 1, 256), F32),
            pltpu.VMEM((1, 256), F32),
            pltpu.VMEM((15, 1, 256), F32),
            pltpu.VMEM((3, ATOMS), jnp.int32),
            pltpu.VMEM((3, ATOMS), jnp.int32),
            pltpu.VMEM((3, ATOMS), F32),
            pltpu.VMEM((1, ATOMS), F32),
            pltpu.VMEM((1, ATOMS), jnp.int32),
            pltpu.SemaphoreType.DMA((2, 15)),
            pltpu.SemaphoreType.DMA((7,)),
        ],
        compiler_params=pltpu.CompilerParams(
            collective_id=0, has_side_effects=True, vmem_limit_bytes=40 * 1024 * 1024
        ),
    )(*[pltpu.with_memory_space_constraint(v, pltpu.HBM) for v in operands])
    hbm = pl.BlockSpec(memory_space=pltpu.HBM)
    return pl.pallas_call(
        store,
        out_shape=(
            jax.ShapeDtypeStruct((CR, CA, CZ), F32),
            jax.ShapeDtypeStruct((3, 4), F32),
        ),
        in_specs=[whole] * 2,
        out_specs=(hbm, hbm),
        scratch_shapes=[pltpu.SemaphoreType.DMA((2,))],
    )(*[pltpu.with_memory_space_constraint(v, pltpu.VMEM) for v in (potential, forces)])


def solution(mesh):
    placed = (P("rad", "ang", "ax"), P("rad", "ang", "ax"), P(), P(), P(), P(), P())
    return jax.shard_map(
        shards,
        mesh=mesh,
        in_specs=placed,
        out_specs=(P("rad", "ang", "ax"), P(None, ("rad", "ang", "ax"))),
        check_vma=False,
    )
```

```python
import functools
import math

import jax
import jax.numpy as jnp
from jax import lax
from jax.experimental import pallas as pl
from jax.experimental.pallas import tpu as pltpu
from jax.sharding import PartitionSpec as P

SWEEPS = 3
GHOST = 3
CR, CA, CZ = 16, 48, 128
N_RAD, N_ANG, N_AX = 8, 32, 2
ROWS = CA + 8
FIRST = 4
PLANES = CR + 2 * GHOST
SLOTS = 256
ATOMS = 2048
MESH = pl.DeviceIdType.MESH
F32, BF16 = jnp.float32, jnp.bfloat16

cheb_low = 0.2
cheb_high = 2.0


def sweep_weights(total_sweeps):
    middle = 0.5 * (cheb_high + cheb_low)
    spread = 0.5 * (cheb_high - cheb_low)
    return [
        1.0 / (middle + spread * math.cos(math.pi * (2 * number + 1) / (2 * total_sweeps)))
        for number in range(total_sweeps)
    ]


def far_first(count):
    return sorted(range(1, count), key=lambda d: -min(d, count - d))


def plane_peers(r, a, x):
    me_x, z_hi, z_lo, me_y = r // 2, lax.rem(r, 2), a // 8, lax.rem(a, 8)
    order = [(dx, dy) for dx in range(4) for dy in range(8) if dx or dy]
    order.sort(key=lambda d: -(min(d[0], 4 - d[0]) + min(d[1], 8 - d[1])))
    for dx, dy in order:
        tx, ty = lax.rem(me_x + dx, 4), lax.rem(me_y + dy, 8)
        yield dx * 8 + dy, (tx * 2 + z_hi, z_lo * 8 + ty, x), tx * 8 + ty


def column_peers(r, a, x):
    me_x, me_y = r // 2, lax.rem(a, 8)
    me = (lax.rem(r, 2) * 4 + a // 8) * 2 + x
    for d in far_first(16):
        t = lax.rem(me + d, 16)
        tz = t // 2
        yield d, (me_x * 2 + tz // 4, lax.rem(tz, 4) * 8 + me_y, lax.rem(t, 2))


def split2(value):
    high = value.astype(BF16)
    return high, (value - high.astype(F32)).astype(BF16)


def split3(value):
    parts = []
    for _ in range(3):
        part = value.astype(BF16).astype(F32)
        parts.append(part)
        value = value - part
    return parts


def shape_pair(distance, valid, width):
    profile = jnp.where(valid, jnp.exp(-(distance * distance) / (2.0 * width * width)), 0.0)
    return profile, profile * (-distance / (width * width))


def iota(shape, dim):
    return lax.broadcasted_iota(jnp.int32, shape, dim)


def nt(left, right):
    return lax.dot_general(left, right, (((1,), (1,)), ((), ())), preferred_element_type=F32)


def slot_table(r, a, x, anchor_ref, extent_ref, center_ref, charge_ref, place_ref):
    anchor = [anchor_ref[d : d + 1, :] for d in range(3)]
    extent = [extent_ref[d : d + 1, :] for d in range(3)]
    back_r = r - anchor[0]
    back_a = (a - anchor[1]) & (N_ANG - 1)
    back_x = (x - anchor[2]) & (N_AX - 1)
    near = (
        (back_r >= -1) & (back_r <= extent[0]) & (((back_a + 1) & (N_ANG - 1)) <= extent[1] + 1)
    )
    mask = jnp.where(near, 1.0, 0.0)
    chunks = ATOMS // 128
    rows = jnp.concatenate([mask[:, 128 * k : 128 * (k + 1)] for k in range(chunks)], axis=0)
    rows16 = rows.astype(BF16)
    before = jnp.where(iota((128, 128), 0) < iota((128, 128), 1), 1.0, 0.0).astype(BF16)
    above = jnp.where(iota((chunks, chunks), 1) < iota((chunks, chunks), 0), 1.0, 0.0).astype(BF16)
    rank = jnp.dot(rows16, before, preferred_element_type=F32)
    rank = rank + jnp.sum(jnp.dot(above, rows16, preferred_element_type=F32), axis=1, keepdims=True)
    rank = jnp.where(rows > 0.5, rank, -1.0)
    slot = iota((SLOTS, 128), 0).astype(F32)
    pick = jnp.concatenate(
        [
            jnp.where(jnp.broadcast_to(rank[k : k + 1, :], (SLOTS, 128)) == slot, 1.0, 0.0).astype(BF16)
            for k in range(chunks)
        ],
        axis=1,
    )
    data = []
    for d, cells in enumerate((CR, CA, CZ)):
        data += split3(center_ref[d : d + 1, :] - (anchor[d] * cells).astype(F32))
    data += split3(charge_ref[...])
    place = place_ref[...]
    data += [v.astype(F32) for v in (back_r, back_a, back_x, *extent)]
    data.append((((place >> 9) * 8) + ((place >> 3) & 7)).astype(F32))
    data.append(
        (((place >> 8) & 1) * 32 + ((place >> 6) & 3) * 8 + (place & 7)).astype(F32)
    )
    data += [jnp.zeros((1, ATOMS), F32)] * 4
    table = nt(pick, jnp.concatenate(data, axis=0).astype(BF16))
    return table.T


def kernel(
    start_hbm,
    source_hbm,
    anchor_hbm,
    extent_hbm,
    center_hbm,
    charge_hbm,
    place_hbm,
    out_ref,
    force_ref,
    va,
    vax,
    vb,
    vbx,
    src,
    coef,
    shape_r,
    ax_in,
    full,
    edge,
    rad_in,
    ang_in,
    corner_in,
    part,
    plane_in,
    mine,
    column_in,
    anchor_ref,
    extent_ref,
    center_ref,
    charge_ref,
    place_ref,
    sems,
    in_sems,
):
    r, a, x = lax.axis_index("rad"), lax.axis_index("ang"), lax.axis_index("ax")
    up, down = lax.rem(r + 1, N_RAD), lax.rem(r + N_RAD - 1, N_RAD)
    nxt, prv = lax.rem(a + 1, N_ANG), lax.rem(a + N_ANG - 1, N_ANG)
    plane = list(plane_peers(r, a, x))
    column = list(column_peers(r, a, x))
    around = [(up, a, x), (down, a, x), (r, nxt, x), (r, prv, x)]
    around += [(up, nxt, x), (down, nxt, x), (up, prv, x), (down, prv, x)]

    barrier = pltpu.get_barrier_semaphore()
    targets = around + [p[1] for p in column] + [p[1] for p in plane]
    for target in targets:
        pl.semaphore_signal(barrier, inc=1, device_id=target, device_id_type=MESH)

    cells = (pl.ds(4, CR), pl.ds(8, CA))
    window = pl.ds(FIRST, ROWS)
    fetch = [
        (start_hbm, va.at[cells]),
        (source_hbm, src.at[cells]),
        (anchor_hbm, anchor_ref),
        (extent_hbm, extent_ref),
        (center_hbm, center_ref),
        (charge_hbm, charge_ref),
        (place_hbm, place_ref),
    ]
    fetch = [pltpu.make_async_copy(*pair, in_sems.at[k]) for k, pair in enumerate(fetch)]
    for copy in fetch:
        copy.start()

    strip = jnp.zeros((PLANES + 2, 8, CZ), F32)
    for ref in (va, vax, vb, vbx, src):
        ref[:, 0:8, :] = strip
        ref[:, 56:64, :] = strip
    empty = jnp.zeros((CA, CZ), F32)
    for p in (0, 1, 2, 3, 20, 21, 22, 23):
        va[p, 8:56] = empty
    for p in (0, 1, 22, 23):
        vax[p, 8:56] = empty
    for p in (1, 2, 21, 22):
        vb[p, 8:56] = empty
        vbx[p, 8:56] = empty

    step = 2.0 * math.pi / (CA * N_ANG)
    index = r * CR + iota((24, CZ), 0) - 4
    radius = 0.5 * (CR * N_RAD) + index.astype(F32) + 0.5
    inside = (index >= 0) & (index < CR * N_RAD)
    upper, lower = (radius + 0.5) / radius, (radius - 0.5) / radius
    angular = 1.0 / (radius * radius * (step * step))
    inverse = jnp.where(inside, 1.0 / (upper + lower + 2.0 * angular + 2.0), 0.0)
    coef[0] = inverse
    coef[1] = inverse * upper
    coef[2] = inverse * lower
    coef[3] = inverse * angular

    for copy in fetch:
        copy.wait()

    lane = iota((ROWS, CZ), 1)
    first, last = lane == 0, lane == CZ - 1
    buffers = [(va, vax), (vb, vbx)]
    for number, weight in enumerate(sweep_weights(SWEEPS)):
        (own, other), (own_new, other_new) = buffers[number % 2], buffers[1 - number % 2]
        for p in range(3 - number, 5 + CR + number):
            c = [jnp.broadcast_to(weight * coef[k, p : p + 1, :], (ROWS, CZ)) for k in range(4)]
            v = own[p, window]
            v_next, v_prev = pltpu.roll(v, CZ - 1, 1), pltpu.roll(v, 1, 1)
            if number == 0:
                along = jnp.where(last, 0.0, v_next) + jnp.where(first, 0.0, v_prev)
                across = jnp.where(last, v_next, 0.0) + jnp.where(first, v_prev, 0.0)
                other_new[p, window] = c[0] * across
            else:
                w = other[p, window]
                w_next, w_prev = pltpu.roll(w, CZ - 1, 1), pltpu.roll(w, 1, 1)
                along = jnp.where(last, w_next, v_next) + jnp.where(first, w_prev, v_prev)
                across = jnp.where(last, v_next, w_next) + jnp.where(first, v_prev, w_prev)
                turn = other[p, pl.ds(FIRST + 1, ROWS)] + other[p, pl.ds(FIRST - 1, ROWS)]
                applied = c[0] * across + c[1] * other[p + 1, window] + c[2] * other[p - 1, window] + c[3] * turn
                other_new[p, window] = (1.0 - weight) * w + applied
            if 4 <= p < 4 + CR:
                along = along + src[p, window]
            turn = own[p, pl.ds(FIRST + 1, ROWS)] + own[p, pl.ds(FIRST - 1, ROWS)]
            applied = c[0] * along + c[1] * own[p + 1, window] + c[2] * own[p - 1, window] + c[3] * turn
            own_new[p, window] = (1.0 - weight) * v + applied
    own, other = buffers[SWEEPS % 2]

    table = slot_table(r, a, x, anchor_ref, extent_ref, center_ref, charge_ref, place_ref)

    def entry(k):
        return table[k : k + 1, :]

    centre = [entry(3 * d) + entry(3 * d + 1) + entry(3 * d + 2) for d in range(3)]
    charge = entry(9) + entry(10) + entry(11)
    back, span = [entry(12 + d) for d in range(3)], [entry(15 + d) for d in range(3)]
    width = (CR / 3.0, CA / 3.0, CZ / 3.0)
    amplitude = 1.0 / math.sqrt(width[1] * width[2] / width[0])

    cell = iota((24, SLOTS), 0).astype(F32) - GHOST
    d = cell + back[0] * CR
    profile, slope = shape_pair(d - centre[0], (d >= 0.0) & (d < span[0] * CR), width[0])
    arc = step * (0.5 * (CR * N_RAD) + (r * CR).astype(F32) + cell + 0.5)
    shape_r[0] = arc * slope
    shape_r[1] = profile
    shape_r[2] = arc * profile

    d = iota((ROWS, SLOTS), 0).astype(F32) - FIRST + back[1] * CA
    d = jnp.where(d < 0.0, d + CA * N_ANG, d)
    d = jnp.where(d >= CA * N_ANG, d - CA * N_ANG, d)
    ang_profile, ang_slope = shape_pair(d - centre[1], d < span[1] * CA, width[1])

    d = iota((2 * CZ, SLOTS), 0).astype(F32) + back[2] * CZ
    d = jnp.where(d >= CZ * N_AX, d - CZ * N_AX, d)
    ax_profile, ax_slope = shape_pair(d - centre[2], d < span[2] * CZ, width[2])
    ax_high, ax_low = split2(jnp.concatenate([ax_profile, ax_slope], axis=1))
    ax_factors = jnp.concatenate([ax_high, ax_high, ax_low], axis=0)


    sums = [jnp.zeros((8, SLOTS), F32) for _ in range(3)]

    def project(first_plane, per):
        block = jnp.concatenate(
            [ref[pl.ds(1 + first_plane, per), window].reshape(per * ROWS, CZ) for ref in (own, other)],
            axis=1,
        )
        high, low = split2(block)
        projected = jnp.dot(
            jnp.concatenate([high, low, high], axis=1), ax_factors, preferred_element_type=F32
        )
        for p in range(per):
            along = [jnp.zeros((8, SLOTS), F32)] * 3
            for t in range(ROWS // 8):
                top = p * ROWS + 8 * t
                plain, sloped = projected[top : top + 8, :SLOTS], projected[top : top + 8, SLOTS:]
                ang_p, ang_s = ang_profile[8 * t : 8 * t + 8], ang_slope[8 * t : 8 * t + 8]
                along = [along[0] + plain * ang_p, along[1] + plain * ang_s, along[2] + sloped * ang_p]
            for k in range(3):
                row = first_plane + p
                sums[k] = sums[k] + shape_r[k, row : row + 1, :] * along[k]

    project(0, 11)
    project(11, 11)

    strength = charge * amplitude
    force = [jnp.sum(s, axis=0, keepdims=True) * strength for s in sums]

    target, low = entry(18), entry(19)
    to = jnp.where(iota((32, SLOTS), 0).astype(F32) == target, 1.0, 0.0).astype(BF16)
    here = iota((64, SLOTS), 0).astype(F32) == low
    spread = jnp.concatenate([jnp.where(here, f, 0.0) for f in force] + [jnp.zeros((64, SLOTS), F32)], axis=0)
    placed = jnp.zeros((32, 256), F32)
    for piece in split3(spread):
        placed = placed + nt(to, piece.astype(BF16))
    for k in range(32):
        part[k] = placed[k : k + 1, :]

    pl.semaphore_wait(barrier, len(targets))

    def send(source, landing, number, device):
        copy = pltpu.make_async_remote_copy(
            src_ref=source,
            dst_ref=landing,
            send_sem=sems.at[0, number],
            recv_sem=sems.at[1, number],
            device_id=device,
            device_id_type=MESH,
        )
        copy.start()
        return copy

    def wait(ref, side, number):
        pltpu.make_async_copy(ref, ref, sems.at[side, number]).wait()

    for slot, device, place in plane:
        send(part.at[place], plane_in.at[slot - 1], 1, device)
    rows = pl.ds(8, CA)
    far = [
        send(own.at[22, rows], rad_in.at[0, 2], 2, around[0]),
        send(own.at[1, rows], rad_in.at[1, 0], 3, around[1]),
    ]
    partner = (r, a, 1 - x)
    below, above, inner = pl.ds(2, 2), pl.ds(20, 2), pl.ds(4, CR)
    ax_copies = [
        send(other.at[planes], ax_in.at[planes], number, partner)
        for planes, number in ((above, 0), (below, 11), (inner, 12))
    ]

    def join(p):
        full[p] = own[p, 8:56] + ax_in[p, 8:56]
        edge[0, p] = own[p, 56:60] + ax_in[p, 56:60]
        edge[1, p] = own[p, 4:8] + ax_in[p, 4:8]

    ax_copies[0].wait_recv()
    join(20)
    join(21)
    near = [send(full.at[above], rad_in.at[0, pl.ds(0, 2)], 13, around[0])]
    ax_copies[1].wait_recv()
    join(2)
    join(3)
    near.append(send(full.at[below], rad_in.at[1, pl.ds(1, 2)], 14, around[1]))
    copies = [
        send(edge.at[0, above], corner_in.at[0], 6, around[4]),
        send(edge.at[0, below], corner_in.at[1], 7, around[5]),
        send(edge.at[1, above], corner_in.at[2], 8, around[6]),
        send(edge.at[1, below], corner_in.at[3], 9, around[7]),
    ]
    ax_copies[2].wait_recv()
    for p in range(4, 4 + CR):
        join(p)
    copies.append(send(edge.at[0, inner], ang_in.at[0], 4, around[2]))
    copies.append(send(edge.at[1, inner], ang_in.at[1], 5, around[3]))
    out_ref[...] = full[inner]

    wait(plane_in, 1, 1)
    me_place = (r // 2) * 8 + lax.rem(a, 8)
    mine[...] = part[me_place] + jnp.sum(plane_in[...], axis=0)
    for slot, device in column:
        send(mine, column_in.at[slot - 1], 10, device)

    for copy in copies:
        copy.wait()
    out_ref[:, 0:4, :] = out_ref[:, 0:4, :] + ang_in[0]
    out_ref[:, CA - 4 : CA, :] = out_ref[:, CA - 4 : CA, :] + ang_in[1]
    for k in range(4):
        planes = pl.ds(14 * (k % 2), 2)
        rows = pl.ds((CA - 4) * (k // 2), 4)
        out_ref[planes, rows, :] = out_ref[planes, rows, :] + corner_in[k]
    for copy in far + near:
        copy.wait()
    out_ref[0:3] = out_ref[0:3] + rad_in[0]
    out_ref[13:16] = out_ref[13:16] + rad_in[1]
    for copy in ax_copies:
        copy.wait_send()

    wait(column_in, 1, 10)
    total = mine[...] + jnp.sum(column_in[...], axis=0)
    me_column = (lax.rem(r, 2) * 4 + a // 8) * 2 + x
    for k in range(3):
        turned = pltpu.roll(jnp.broadcast_to(total, (8, 256)), lax.rem(512 - 64 * k - 4 * me_column, 256), 1)
        force_ref[k : k + 1, :] = turned[0:1, 0:4]
    wait(plane_in, 0, 1)
    wait(column_in, 0, 10)


def store(potential_ref, force_ref, potential_out, force_out, sems):
    copies = [
        pltpu.make_async_copy(potential_ref, potential_out, sems.at[0]),
        pltpu.make_async_copy(force_ref, force_out, sems.at[1]),
    ]
    for copy in copies:
        copy.start()
    for copy in copies:
        copy.wait()


def shards(start_potential, charge_density, box_anchor, box_extent, atom_center, atom_charge, atom_place):
    whole = pl.BlockSpec(memory_space=pltpu.VMEM)
    operands = [start_potential, charge_density, box_anchor, box_extent, atom_center]
    operands += [atom_charge.reshape(1, ATOMS), atom_place.reshape(1, ATOMS)]
    grid = (PLANES + 2, CA + 16, CZ)
    potential, forces = pl.pallas_call(
        kernel,
        out_shape=(
            jax.ShapeDtypeStruct((CR, CA, CZ), F32),
            jax.ShapeDtypeStruct((3, 4), F32),
        ),
        in_specs=[pl.BlockSpec(memory_space=pltpu.HBM)] * 7,
        out_specs=(whole, whole),
        scratch_shapes=[
            *[pltpu.VMEM(grid, F32)] * 5,
            pltpu.VMEM((4, 24, CZ), F32),
            pltpu.VMEM((3, 24, SLOTS), F32),
            pltpu.VMEM(grid, F32),
            pltpu.VMEM((PLANES + 2, CA, CZ), F32),
            pltpu.VMEM((2, PLANES + 2, 4, CZ), F32),
            pltpu.VMEM((2, GHOST, CA, CZ), F32),
            pltpu.VMEM((2, CR, 4, CZ), F32),
            pltpu.VMEM((4, 2, 4, CZ), F32),
            pltpu.VMEM((32, 1, 256), F32),
            pltpu.VMEM((31, 1, 256), F32),
            pltpu.VMEM((1, 256), F32),
            pltpu.VMEM((15, 1, 256), F32),
            pltpu.VMEM((3, ATOMS), jnp.int32),
            pltpu.VMEM((3, ATOMS), jnp.int32),
            pltpu.VMEM((3, ATOMS), F32),
            pltpu.VMEM((1, ATOMS), F32),
            pltpu.VMEM((1, ATOMS), jnp.int32),
            pltpu.SemaphoreType.DMA((2, 15)),
            pltpu.SemaphoreType.DMA((7,)),
        ],
        compiler_params=pltpu.CompilerParams(
            collective_id=0, has_side_effects=True, vmem_limit_bytes=40 * 1024 * 1024
        ),
    )(*[pltpu.with_memory_space_constraint(v, pltpu.HBM) for v in operands])
    hbm = pl.BlockSpec(memory_space=pltpu.HBM)
    return pl.pallas_call(
        store,
        out_shape=(
            jax.ShapeDtypeStruct((CR, CA, CZ), F32),
            jax.ShapeDtypeStruct((3, 4), F32),
        ),
        in_specs=[whole] * 2,
        out_specs=(hbm, hbm),
        scratch_shapes=[pltpu.SemaphoreType.DMA((2,))],
    )(*[pltpu.with_memory_space_constraint(v, pltpu.VMEM) for v in (potential, forces)])


def solution(mesh):
    placed = (P("rad", "ang", "ax"), P("rad", "ang", "ax"), P(), P(), P(), P(), P())
    return jax.shard_map(
        shards,
        mesh=mesh,
        in_specs=placed,
        out_specs=(P("rad", "ang", "ax"), P(None, ("rad", "ang", "ax"))),
        check_vma=False,
    )
```

```python
import functools
import math

import jax
import jax.numpy as jnp
from jax import lax
from jax.experimental import pallas as pl
from jax.experimental.pallas import tpu as pltpu
from jax.sharding import PartitionSpec as P

SWEEPS = 3
GHOST = 3
CR, CA, CZ = 16, 48, 128
N_RAD, N_ANG, N_AX = 8, 32, 2
ROWS = CA + 8
FIRST = 4
PLANES = CR + 2 * GHOST
SLOTS = 256
ATOMS = 2048
MESH = pl.DeviceIdType.MESH
F32, BF16 = jnp.float32, jnp.bfloat16

cheb_low = 0.2
cheb_high = 2.0


def sweep_weights(total_sweeps):
    middle = 0.5 * (cheb_high + cheb_low)
    spread = 0.5 * (cheb_high - cheb_low)
    return [
        1.0 / (middle + spread * math.cos(math.pi * (2 * number + 1) / (2 * total_sweeps)))
        for number in range(total_sweeps)
    ]


def plane_peers(r, a, x):
    me_x, z_hi, z_lo, me_y = r // 2, lax.rem(r, 2), a // 8, lax.rem(a, 8)
    order = [(dx, dy) for dx in range(4) for dy in range(8) if dx or dy]
    order.sort(key=lambda d: -(min(d[0], 4 - d[0]) + min(d[1], 8 - d[1])))
    for dx, dy in order:
        tx, ty = lax.rem(me_x + dx, 4), lax.rem(me_y + dy, 8)
        yield dx * 8 + dy, (tx * 2 + z_hi, z_lo * 8 + ty, x), tx * 8 + ty


def column_peers(r, a, x):
    z_hi, z_lo, me_y = lax.rem(r, 2), a // 8, lax.rem(a, 8)
    for flip in (1, 0):
        for d in (0, 4, 3, 5, 2, 6, 1, 7):
            if flip or d:
                t = lax.rem(z_lo * 2 + x + d, 8)
                half = 1 - z_hi if flip else z_hi
                yield 8 * flip + d, ((r // 2) * 2 + half, (t // 2) * 8 + me_y, lax.rem(t, 2))


def split2(value):
    high = value.astype(BF16)
    return high, (value - high.astype(F32)).astype(BF16)


def split3(value):
    parts = []
    for _ in range(3):
        part = value.astype(BF16).astype(F32)
        parts.append(part)
        value = value - part
    return parts


def shape_pair(distance, valid, width):
    profile = jnp.where(valid, jnp.exp(-(distance * distance) / (2.0 * width * width)), 0.0)
    return profile, profile * (-distance / (width * width))


def iota(shape, dim):
    return lax.broadcasted_iota(jnp.int32, shape, dim)


def nt(left, right):
    return lax.dot_general(left, right, (((1,), (1,)), ((), ())), preferred_element_type=F32)


def slot_table(r, a, x, anchor_ref, extent_ref, center_ref, charge_ref, place_ref):
    anchor = [anchor_ref[d : d + 1, :] for d in range(3)]
    extent = [extent_ref[d : d + 1, :] for d in range(3)]
    back_r = r - anchor[0]
    back_a = (a - anchor[1]) & (N_ANG - 1)
    back_x = (x - anchor[2]) & (N_AX - 1)
    near = (
        (back_r >= -1) & (back_r <= extent[0]) & (((back_a + 1) & (N_ANG - 1)) <= extent[1] + 1)
    )
    mask = jnp.where(near, 1.0, 0.0)
    chunks = ATOMS // 128
    rows = jnp.concatenate([mask[:, 128 * k : 128 * (k + 1)] for k in range(chunks)], axis=0)
    rows16 = rows.astype(BF16)
    before = jnp.where(iota((128, 128), 0) < iota((128, 128), 1), 1.0, 0.0).astype(BF16)
    above = jnp.where(iota((chunks, chunks), 1) < iota((chunks, chunks), 0), 1.0, 0.0).astype(BF16)
    rank = jnp.dot(rows16, before, preferred_element_type=F32)
    rank = rank + jnp.sum(jnp.dot(above, rows16, preferred_element_type=F32), axis=1, keepdims=True)
    rank = jnp.where(rows > 0.5, rank, -1.0)
    slot = iota((SLOTS, 128), 0).astype(F32)
    pick = jnp.concatenate(
        [
            jnp.where(jnp.broadcast_to(rank[k : k + 1, :], (SLOTS, 128)) == slot, 1.0, 0.0).astype(BF16)
            for k in range(chunks)
        ],
        axis=1,
    )
    data = []
    for d, cells in enumerate((CR, CA, CZ)):
        data += split3(center_ref[d : d + 1, :] - (anchor[d] * cells).astype(F32))
    data += split3(charge_ref[...])
    place = place_ref[...]
    data += [v.astype(F32) for v in (back_r, back_a, back_x, *extent)]
    data.append((((place >> 9) * 8) + ((place >> 3) & 7)).astype(F32))
    data.append(
        (((place >> 8) & 1) * 32 + ((place >> 6) & 3) * 8 + (place & 7)).astype(F32)
    )
    data += [jnp.zeros((1, ATOMS), F32)] * 4
    table = nt(pick, jnp.concatenate(data, axis=0).astype(BF16))
    return table.T


def kernel(
    start_hbm,
    source_hbm,
    anchor_hbm,
    extent_hbm,
    center_hbm,
    charge_hbm,
    place_hbm,
    out_ref,
    force_ref,
    va,
    vax,
    vb,
    vbx,
    src,
    coef,
    shape_r,
    ax_in,
    full,
    edge,
    rad_in,
    ang_in,
    corner_in,
    part,
    plane_in,
    mine,
    column_in,
    anchor_ref,
    extent_ref,
    center_ref,
    charge_ref,
    place_ref,
    ready,
    sems,
    in_sems,
):
    cells = (pl.ds(4, CR), pl.ds(8, CA))
    window = pl.ds(FIRST, ROWS)
    fetch = [
        (start_hbm, va.at[cells]),
        (source_hbm, src.at[cells]),
        (anchor_hbm, anchor_ref),
        (extent_hbm, extent_ref),
        (center_hbm, center_ref),
        (charge_hbm, charge_ref),
        (place_hbm, place_ref),
    ]
    fetch = [pltpu.make_async_copy(*pair, in_sems.at[k]) for k, pair in enumerate(fetch)]
    for copy in fetch:
        copy.start()

    r, a, x = lax.axis_index("rad"), lax.axis_index("ang"), lax.axis_index("ax")
    up, down = lax.rem(r + 1, N_RAD), lax.rem(r + N_RAD - 1, N_RAD)
    nxt, prv = lax.rem(a + 1, N_ANG), lax.rem(a + N_ANG - 1, N_ANG)
    plane = list(plane_peers(r, a, x))
    column = list(column_peers(r, a, x))
    around = [(up, a, x), (down, a, x), (r, nxt, x), (r, prv, x)]
    around += [(up, nxt, x), (down, nxt, x), (up, prv, x), (down, prv, x)]

    barrier = pltpu.get_barrier_semaphore()
    far_column = [device for slot, device in column if slot >= 8]
    targets = around + [device for slot, device in column if slot < 8] + [p[1] for p in plane]
    odd = lax.rem(r, 2)
    for target in targets:
        pl.semaphore_signal(barrier, inc=1, device_id=target, device_id_type=MESH)

    @pl.when(odd == 0)
    def _():
        for target in far_column:
            pl.semaphore_signal(barrier, inc=1, device_id=target, device_id_type=MESH)


    strip = jnp.zeros((PLANES + 2, 8, CZ), F32)
    for ref in (va, vax, vb, vbx, src):
        ref[:, 0:8, :] = strip
        ref[:, 56:64, :] = strip
    empty = jnp.zeros((CA, CZ), F32)
    for p in (0, 1, 2, 3, 20, 21, 22, 23):
        va[p, 8:56] = empty
    for p in (0, 1, 22, 23):
        vax[p, 8:56] = empty
    for p in (1, 2, 21, 22):
        vb[p, 8:56] = empty
        vbx[p, 8:56] = empty

    step = 2.0 * math.pi / (CA * N_ANG)
    index = r * CR + iota((24, CZ), 0) - 4
    radius = 0.5 * (CR * N_RAD) + index.astype(F32) + 0.5
    inside = (index >= 0) & (index < CR * N_RAD)
    upper, lower = (radius + 0.5) / radius, (radius - 0.5) / radius
    angular = 1.0 / (radius * radius * (step * step))
    inverse = jnp.where(inside, 1.0 / (upper + lower + 2.0 * angular + 2.0), 0.0)
    coef[0] = inverse
    coef[1] = inverse * upper
    coef[2] = inverse * lower
    coef[3] = inverse * angular

    for copy in fetch:
        copy.wait()

    lane = iota((ROWS, CZ), 1)
    first, last = lane == 0, lane == CZ - 1
    buffers = [(va, vax), (vb, vbx)]
    for number, weight in enumerate(sweep_weights(SWEEPS)):
        (own, other), (own_new, other_new) = buffers[number % 2], buffers[1 - number % 2]
        for p in range(3 - number, 5 + CR + number):
            c = [jnp.broadcast_to(weight * coef[k, p : p + 1, :], (ROWS, CZ)) for k in range(4)]
            v = own[p, window]
            v_next, v_prev = pltpu.roll(v, CZ - 1, 1), pltpu.roll(v, 1, 1)
            if number == 0:
                along = jnp.where(last, 0.0, v_next) + jnp.where(first, 0.0, v_prev)
                across = jnp.where(last, v_next, 0.0) + jnp.where(first, v_prev, 0.0)
                other_new[p, window] = c[0] * across
            else:
                w = other[p, window]
                w_next, w_prev = pltpu.roll(w, CZ - 1, 1), pltpu.roll(w, 1, 1)
                along = jnp.where(last, w_next, v_next) + jnp.where(first, w_prev, v_prev)
                across = jnp.where(last, v_next, w_next) + jnp.where(first, v_prev, w_prev)
                turn = other[p, pl.ds(FIRST + 1, ROWS)] + other[p, pl.ds(FIRST - 1, ROWS)]
                applied = c[0] * across + c[1] * other[p + 1, window] + c[2] * other[p - 1, window] + c[3] * turn
                other_new[p, window] = (1.0 - weight) * w + applied
            if 4 <= p < 4 + CR:
                along = along + src[p, window]
            turn = own[p, pl.ds(FIRST + 1, ROWS)] + own[p, pl.ds(FIRST - 1, ROWS)]
            applied = c[0] * along + c[1] * own[p + 1, window] + c[2] * own[p - 1, window] + c[3] * turn
            own_new[p, window] = (1.0 - weight) * v + applied
    own, other = buffers[SWEEPS % 2]

    table = slot_table(r, a, x, anchor_ref, extent_ref, center_ref, charge_ref, place_ref)

    def entry(k):
        return table[k : k + 1, :]

    centre = [entry(3 * d) + entry(3 * d + 1) + entry(3 * d + 2) for d in range(3)]
    charge = entry(9) + entry(10) + entry(11)
    back, span = [entry(12 + d) for d in range(3)], [entry(15 + d) for d in range(3)]
    width = (CR / 3.0, CA / 3.0, CZ / 3.0)
    amplitude = 1.0 / math.sqrt(width[1] * width[2] / width[0])

    cell = iota((24, SLOTS), 0).astype(F32) - GHOST
    d = cell + back[0] * CR
    profile, slope = shape_pair(d - centre[0], (d >= 0.0) & (d < span[0] * CR), width[0])
    arc = step * (0.5 * (CR * N_RAD) + (r * CR).astype(F32) + cell + 0.5)
    shape_r[0] = arc * slope
    shape_r[1] = profile
    shape_r[2] = arc * profile

    d = iota((ROWS, SLOTS), 0).astype(F32) - FIRST + back[1] * CA
    d = jnp.where(d < 0.0, d + CA * N_ANG, d)
    d = jnp.where(d >= CA * N_ANG, d - CA * N_ANG, d)
    ang_profile, ang_slope = shape_pair(d - centre[1], d < span[1] * CA, width[1])

    d = iota((2 * CZ, SLOTS), 0).astype(F32) + back[2] * CZ
    d = jnp.where(d >= CZ * N_AX, d - CZ * N_AX, d)
    ax_profile, ax_slope = shape_pair(d - centre[2], d < span[2] * CZ, width[2])
    ax_high, ax_low = split2(jnp.concatenate([ax_profile, ax_slope], axis=1))
    ax_factors = jnp.concatenate([ax_high, ax_high, ax_low], axis=0)


    sums = [jnp.zeros((8, SLOTS), F32) for _ in range(3)]

    def project(first_plane, per):
        block = jnp.concatenate(
            [ref[pl.ds(1 + first_plane, per), window].reshape(per * ROWS, CZ) for ref in (own, other)],
            axis=1,
        )
        high, low = split2(block)
        projected = jnp.dot(
            jnp.concatenate([high, low, high], axis=1), ax_factors, preferred_element_type=F32
        )
        for p in range(per):
            along = [jnp.zeros((8, SLOTS), F32)] * 3
            for t in range(ROWS // 8):
                top = p * ROWS + 8 * t
                plain, sloped = projected[top : top + 8, :SLOTS], projected[top : top + 8, SLOTS:]
                ang_p, ang_s = ang_profile[8 * t : 8 * t + 8], ang_slope[8 * t : 8 * t + 8]
                along = [along[0] + plain * ang_p, along[1] + plain * ang_s, along[2] + sloped * ang_p]
            for k in range(3):
                row = first_plane + p
                sums[k] = sums[k] + shape_r[k, row : row + 1, :] * along[k]

    project(0, 11)
    project(11, 11)

    strength = charge * amplitude
    force = [jnp.sum(s, axis=0, keepdims=True) * strength for s in sums]

    target, low = entry(18), entry(19)
    to = jnp.where(iota((32, SLOTS), 0).astype(F32) == target, 1.0, 0.0).astype(BF16)
    here = iota((64, SLOTS), 0).astype(F32) == low
    spread = jnp.concatenate([jnp.where(here, f, 0.0) for f in force] + [jnp.zeros((64, SLOTS), F32)], axis=0)
    placed = jnp.zeros((32, 256), F32)
    for piece in split2(spread):
        placed = placed + nt(to, piece)
    for k in range(32):
        part[k] = placed[k : k + 1, :]

    pl.semaphore_wait(barrier, len(targets) + odd * len(far_column))

    @pl.when(odd == 1)
    def _():
        for target in far_column:
            pl.semaphore_signal(ready, inc=1, device_id=target, device_id_type=MESH)


    def send(source, landing, number, device):
        copy = pltpu.make_async_remote_copy(
            src_ref=source,
            dst_ref=landing,
            send_sem=sems.at[0, number],
            recv_sem=sems.at[1, number],
            device_id=device,
            device_id_type=MESH,
        )
        copy.start()
        return copy

    def wait(ref, side, number):
        pltpu.make_async_copy(ref, ref, sems.at[side, number]).wait()

    for slot, device, place in plane:
        send(part.at[place], plane_in.at[slot - 1], 1, device)
    rows = pl.ds(8, CA)
    far = [
        send(own.at[22, rows], rad_in.at[0, 2], 2, around[0]),
        send(own.at[1, rows], rad_in.at[1, 0], 3, around[1]),
    ]
    partner = (r, a, 1 - x)
    below, above, inner = pl.ds(2, 2), pl.ds(20, 2), pl.ds(4, CR)
    ax_copies = [
        send(other.at[planes], ax_in.at[planes], number, partner)
        for planes, number in ((above, 0), (below, 11), (inner, 12))
    ]

    def join(p):
        full[p] = own[p, 8:56] + ax_in[p, 8:56]
        edge[0, p] = own[p, 56:60] + ax_in[p, 56:60]
        edge[1, p] = own[p, 4:8] + ax_in[p, 4:8]

    ax_copies[0].wait_recv()
    join(20)
    join(21)
    near = [send(full.at[above], rad_in.at[0, pl.ds(0, 2)], 13, around[0])]
    ax_copies[1].wait_recv()
    join(2)
    join(3)
    near.append(send(full.at[below], rad_in.at[1, pl.ds(1, 2)], 14, around[1]))
    copies = [
        send(edge.at[0, above], corner_in.at[0], 6, around[4]),
        send(edge.at[0, below], corner_in.at[1], 7, around[5]),
        send(edge.at[1, above], corner_in.at[2], 8, around[6]),
        send(edge.at[1, below], corner_in.at[3], 9, around[7]),
    ]
    ax_copies[2].wait_recv()
    for p in range(4, 4 + CR):
        join(p)
    copies.append(send(edge.at[0, inner], ang_in.at[0], 4, around[2]))
    copies.append(send(edge.at[1, inner], ang_in.at[1], 5, around[3]))
    out_ref[...] = full[inner]

    wait(plane_in, 1, 1)
    me_place = (r // 2) * 8 + lax.rem(a, 8)
    mine[...] = part[me_place] + jnp.sum(plane_in[...], axis=0)

    @pl.when(odd == 0)
    def _():
        pl.semaphore_wait(ready, len(far_column))

    for slot, device in column:
        send(mine, column_in.at[slot - 1], 10, device)

    for copy in copies:
        copy.wait()
    out_ref[:, 0:4, :] = out_ref[:, 0:4, :] + ang_in[0]
    out_ref[:, CA - 4 : CA, :] = out_ref[:, CA - 4 : CA, :] + ang_in[1]
    for k in range(4):
        planes = pl.ds(14 * (k % 2), 2)
        rows = pl.ds((CA - 4) * (k // 2), 4)
        out_ref[planes, rows, :] = out_ref[planes, rows, :] + corner_in[k]
    for copy in far + near:
        copy.wait()
    out_ref[0:3] = out_ref[0:3] + rad_in[0]
    out_ref[13:16] = out_ref[13:16] + rad_in[1]
    for copy in ax_copies:
        copy.wait_send()

    wait(column_in, 1, 10)
    total = mine[...] + jnp.sum(column_in[...], axis=0)
    me_column = (lax.rem(r, 2) * 4 + a // 8) * 2 + x
    for k in range(3):
        turned = pltpu.roll(jnp.broadcast_to(total, (8, 256)), lax.rem(512 - 64 * k - 4 * me_column, 256), 1)
        force_ref[k : k + 1, :] = turned[0:1, 0:4]
    wait(plane_in, 0, 1)
    wait(column_in, 0, 10)


def store(potential_ref, force_ref, potential_out, force_out, sems):
    copies = [
        pltpu.make_async_copy(potential_ref, potential_out, sems.at[0]),
        pltpu.make_async_copy(force_ref, force_out, sems.at[1]),
    ]
    for copy in copies:
        copy.start()
    for copy in copies:
        copy.wait()


def shards(start_potential, charge_density, box_anchor, box_extent, atom_center, atom_charge, atom_place):
    whole = pl.BlockSpec(memory_space=pltpu.VMEM)
    operands = [start_potential, charge_density, box_anchor, box_extent, atom_center]
    operands += [atom_charge.reshape(1, ATOMS), atom_place.reshape(1, ATOMS)]
    grid = (PLANES + 2, CA + 16, CZ)
    potential, forces = pl.pallas_call(
        kernel,
        out_shape=(
            jax.ShapeDtypeStruct((CR, CA, CZ), F32),
            jax.ShapeDtypeStruct((3, 4), F32),
        ),
        in_specs=[pl.BlockSpec(memory_space=pltpu.HBM)] * 7,
        out_specs=(whole, whole),
        scratch_shapes=[
            *[pltpu.VMEM(grid, F32)] * 5,
            pltpu.VMEM((4, 24, CZ), F32),
            pltpu.VMEM((3, 24, SLOTS), F32),
            pltpu.VMEM(grid, F32),
            pltpu.VMEM((PLANES + 2, CA, CZ), F32),
            pltpu.VMEM((2, PLANES + 2, 4, CZ), F32),
            pltpu.VMEM((2, GHOST, CA, CZ), F32),
            pltpu.VMEM((2, CR, 4, CZ), F32),
            pltpu.VMEM((4, 2, 4, CZ), F32),
            pltpu.VMEM((32, 1, 256), F32),
            pltpu.VMEM((31, 1, 256), F32),
            pltpu.VMEM((1, 256), F32),
            pltpu.VMEM((15, 1, 256), F32),
            pltpu.VMEM((3, ATOMS), jnp.int32),
            pltpu.VMEM((3, ATOMS), jnp.int32),
            pltpu.VMEM((3, ATOMS), F32),
            pltpu.VMEM((1, ATOMS), F32),
            pltpu.VMEM((1, ATOMS), jnp.int32),
            pltpu.SemaphoreType.REGULAR,
            pltpu.SemaphoreType.DMA((2, 15)),
            pltpu.SemaphoreType.DMA((7,)),
        ],
        compiler_params=pltpu.CompilerParams(
            collective_id=0, has_side_effects=True, vmem_limit_bytes=40 * 1024 * 1024
        ),
    )(*[pltpu.with_memory_space_constraint(v, pltpu.HBM) for v in operands])
    hbm = pl.BlockSpec(memory_space=pltpu.HBM)
    return pl.pallas_call(
        store,
        out_shape=(
            jax.ShapeDtypeStruct((CR, CA, CZ), F32),
            jax.ShapeDtypeStruct((3, 4), F32),
        ),
        in_specs=[whole] * 2,
        out_specs=(hbm, hbm),
        scratch_shapes=[pltpu.SemaphoreType.DMA((2,))],
    )(*[pltpu.with_memory_space_constraint(v, pltpu.VMEM) for v in (potential, forces)])


def solution(mesh):
    placed = (P("rad", "ang", "ax"), P("rad", "ang", "ax"), P(), P(), P(), P(), P())
    return jax.shard_map(
        shards,
        mesh=mesh,
        in_specs=placed,
        out_specs=(P("rad", "ang", "ax"), P(None, ("rad", "ang", "ax"))),
        check_vma=False,
    )
```

```python
import functools
import math

import jax
import jax.numpy as jnp
from jax import lax
from jax.experimental import pallas as pl
from jax.experimental.pallas import tpu as pltpu
from jax.sharding import PartitionSpec as P

SWEEPS = 3
GHOST = 3
CR, CA, CZ = 16, 48, 128
N_RAD, N_ANG, N_AX = 8, 32, 2
ROWS = CA + 8
FIRST = 4
PLANES = CR + 2 * GHOST
SLOTS = 256
ATOMS = 2048
MESH = pl.DeviceIdType.MESH
F32, BF16 = jnp.float32, jnp.bfloat16

cheb_low = 0.2
cheb_high = 2.0


def sweep_weights(total_sweeps):
    middle = 0.5 * (cheb_high + cheb_low)
    spread = 0.5 * (cheb_high - cheb_low)
    return [
        1.0 / (middle + spread * math.cos(math.pi * (2 * number + 1) / (2 * total_sweeps)))
        for number in range(total_sweeps)
    ]


def plane_peers(r, a, x):
    me_x, z_hi, z_lo, me_y = r // 2, lax.rem(r, 2), a // 8, lax.rem(a, 8)
    order = [(dx, dy) for dx in range(4) for dy in range(8) if dx or dy]
    order.sort(key=lambda d: -(min(d[0], 4 - d[0]) + min(d[1], 8 - d[1])))
    for dx, dy in order:
        tx, ty = lax.rem(me_x + dx, 4), lax.rem(me_y + dy, 8)
        yield dx * 8 + dy, (tx * 2 + z_hi, z_lo * 8 + ty, x), tx * 8 + ty


def column_peers(r, a, x):
    z_hi, z_lo, me_y = lax.rem(r, 2), a // 8, lax.rem(a, 8)
    for flip in (1, 0):
        for d in (0, 4, 3, 5, 2, 6, 1, 7):
            if flip or d:
                t = lax.rem(z_lo * 2 + x + d, 8)
                half = 1 - z_hi if flip else z_hi
                yield 8 * flip + d, ((r // 2) * 2 + half, (t // 2) * 8 + me_y, lax.rem(t, 2))


def split2(value):
    high = value.astype(BF16)
    return high, (value - high.astype(F32)).astype(BF16)


def split3(value):
    parts = []
    for _ in range(3):
        part = value.astype(BF16).astype(F32)
        parts.append(part)
        value = value - part
    return parts


def shape_pair(distance, valid, width):
    profile = jnp.where(valid, jnp.exp(-(distance * distance) / (2.0 * width * width)), 0.0)
    return profile, profile * (-distance / (width * width))


def iota(shape, dim):
    return lax.broadcasted_iota(jnp.int32, shape, dim)


def nt(left, right):
    return lax.dot_general(left, right, (((1,), (1,)), ((), ())), preferred_element_type=F32)


def slot_table(r, a, x, anchor_ref, extent_ref, center_ref, charge_ref, place_ref):
    anchor = [anchor_ref[d : d + 1, :] for d in range(3)]
    extent = [extent_ref[d : d + 1, :] for d in range(3)]
    back_r = r - anchor[0]
    back_a = (a - anchor[1]) & (N_ANG - 1)
    back_x = (x - anchor[2]) & (N_AX - 1)
    near = (
        (back_r >= -1) & (back_r <= extent[0]) & (((back_a + 1) & (N_ANG - 1)) <= extent[1] + 1)
    )
    mask = jnp.where(near, 1.0, 0.0)
    chunks = ATOMS // 128
    rows = jnp.concatenate([mask[:, 128 * k : 128 * (k + 1)] for k in range(chunks)], axis=0)
    rows16 = rows.astype(BF16)
    before = jnp.where(iota((128, 128), 0) < iota((128, 128), 1), 1.0, 0.0).astype(BF16)
    above = jnp.where(iota((chunks, chunks), 1) < iota((chunks, chunks), 0), 1.0, 0.0).astype(BF16)
    rank = jnp.dot(rows16, before, preferred_element_type=F32)
    rank = rank + jnp.sum(jnp.dot(above, rows16, preferred_element_type=F32), axis=1, keepdims=True)
    rank = jnp.where(rows > 0.5, rank, -1.0)
    slot = iota((SLOTS, 128), 0).astype(F32)
    pick = jnp.concatenate(
        [
            jnp.where(jnp.broadcast_to(rank[k : k + 1, :], (SLOTS, 128)) == slot, 1.0, 0.0).astype(BF16)
            for k in range(chunks)
        ],
        axis=1,
    )
    data = []
    for d, cells in enumerate((CR, CA, CZ)):
        data += split3(center_ref[d : d + 1, :] - (anchor[d] * cells).astype(F32))
    data += split3(charge_ref[...])
    place = place_ref[...]
    data += [v.astype(F32) for v in (back_r, back_a, back_x, *extent)]
    data.append((((place >> 9) * 8) + ((place >> 3) & 7)).astype(F32))
    data.append(
        (((place >> 8) & 1) * 32 + ((place >> 6) & 3) * 8 + (place & 7)).astype(F32)
    )
    data += [jnp.zeros((1, ATOMS), F32)] * 4
    table = nt(pick, jnp.concatenate(data, axis=0).astype(BF16))
    return table.T


def kernel(
    start_hbm,
    source_hbm,
    anchor_hbm,
    extent_hbm,
    center_hbm,
    charge_hbm,
    place_hbm,
    out_ref,
    force_ref,
    va,
    vax,
    vb,
    vbx,
    src,
    coef,
    shape_r,
    ax_in,
    full,
    edge,
    rad_in,
    ang_in,
    corner_in,
    part,
    plane_in,
    mine,
    column_in,
    anchor_ref,
    extent_ref,
    center_ref,
    charge_ref,
    place_ref,
    ready,
    sems,
    in_sems,
):
    cells = (pl.ds(4, CR), pl.ds(8, CA))
    window = pl.ds(FIRST, ROWS)
    fetch = [
        (start_hbm, va.at[cells]),
        (source_hbm, src.at[cells]),
        (anchor_hbm, anchor_ref),
        (extent_hbm, extent_ref),
        (center_hbm, center_ref),
        (charge_hbm, charge_ref),
        (place_hbm, place_ref),
    ]
    fetch = [pltpu.make_async_copy(*pair, in_sems.at[k]) for k, pair in enumerate(fetch)]
    for copy in fetch:
        copy.start()

    r, a, x = lax.axis_index("rad"), lax.axis_index("ang"), lax.axis_index("ax")
    up, down = lax.rem(r + 1, N_RAD), lax.rem(r + N_RAD - 1, N_RAD)
    nxt, prv = lax.rem(a + 1, N_ANG), lax.rem(a + N_ANG - 1, N_ANG)
    plane = list(plane_peers(r, a, x))
    column = list(column_peers(r, a, x))
    around = [(up, a, x), (down, a, x), (r, nxt, x), (r, prv, x)]
    around += [(up, nxt, x), (down, nxt, x), (up, prv, x), (down, prv, x)]

    barrier = pltpu.get_barrier_semaphore()
    far_column = [device for slot, device in column if slot >= 8]
    targets = around + [device for slot, device in column if slot < 8] + [p[1] for p in plane]
    odd = lax.rem(r, 2)
    for target in targets:
        pl.semaphore_signal(barrier, inc=1, device_id=target, device_id_type=MESH)

    @pl.when(odd == 0)
    def _():
        for target in far_column:
            pl.semaphore_signal(barrier, inc=1, device_id=target, device_id_type=MESH)


    strip = jnp.zeros((PLANES + 2, 8, CZ), F32)
    for ref in (va, vax, vb, vbx, src):
        ref[:, 0:8, :] = strip
        ref[:, 56:64, :] = strip
    empty = jnp.zeros((CA, CZ), F32)
    for p in (0, 1, 2, 3, 20, 21, 22, 23):
        va[p, 8:56] = empty
    for p in (0, 1, 22, 23):
        vax[p, 8:56] = empty
    for p in (1, 2, 21, 22):
        vb[p, 8:56] = empty
        vbx[p, 8:56] = empty

    step = 2.0 * math.pi / (CA * N_ANG)
    index = r * CR + iota((24, CZ), 0) - 4
    radius = 0.5 * (CR * N_RAD) + index.astype(F32) + 0.5
    inside = (index >= 0) & (index < CR * N_RAD)
    upper, lower = (radius + 0.5) / radius, (radius - 0.5) / radius
    angular = 1.0 / (radius * radius * (step * step))
    inverse = jnp.where(inside, 1.0 / (upper + lower + 2.0 * angular + 2.0), 0.0)
    coef[0] = inverse
    coef[1] = inverse * upper
    coef[2] = inverse * lower
    coef[3] = inverse * angular

    for copy in fetch:
        copy.wait()

    lane = iota((ROWS, CZ), 1)
    first, last = lane == 0, lane == CZ - 1
    buffers = [(va, vax), (vb, vbx)]
    for number, weight in enumerate(sweep_weights(SWEEPS)):
        (own, other), (own_new, other_new) = buffers[number % 2], buffers[1 - number % 2]
        for p in range(3 - number, 5 + CR + number):
            c = [jnp.broadcast_to(weight * coef[k, p : p + 1, :], (ROWS, CZ)) for k in range(4)]
            v = own[p, window]
            v_next, v_prev = pltpu.roll(v, CZ - 1, 1), pltpu.roll(v, 1, 1)
            if number == 0:
                along = jnp.where(last, 0.0, v_next) + jnp.where(first, 0.0, v_prev)
                across = jnp.where(last, v_next, 0.0) + jnp.where(first, v_prev, 0.0)
                other_new[p, window] = c[0] * across
            else:
                w = other[p, window]
                w_next, w_prev = pltpu.roll(w, CZ - 1, 1), pltpu.roll(w, 1, 1)
                along = jnp.where(last, w_next, v_next) + jnp.where(first, w_prev, v_prev)
                across = jnp.where(last, v_next, w_next) + jnp.where(first, v_prev, w_prev)
                turn = other[p, pl.ds(FIRST + 1, ROWS)] + other[p, pl.ds(FIRST - 1, ROWS)]
                applied = c[0] * across + c[1] * other[p + 1, window] + c[2] * other[p - 1, window] + c[3] * turn
                other_new[p, window] = (1.0 - weight) * w + applied
            if 4 <= p < 4 + CR:
                along = along + src[p, window]
            turn = own[p, pl.ds(FIRST + 1, ROWS)] + own[p, pl.ds(FIRST - 1, ROWS)]
            applied = c[0] * along + c[1] * own[p + 1, window] + c[2] * own[p - 1, window] + c[3] * turn
            own_new[p, window] = (1.0 - weight) * v + applied
    own, other = buffers[SWEEPS % 2]

    table = slot_table(r, a, x, anchor_ref, extent_ref, center_ref, charge_ref, place_ref)

    def entry(k):
        return table[k : k + 1, :]

    centre = [entry(3 * d) + entry(3 * d + 1) + entry(3 * d + 2) for d in range(3)]
    charge = entry(9) + entry(10) + entry(11)
    back, span = [entry(12 + d) for d in range(3)], [entry(15 + d) for d in range(3)]
    width = (CR / 3.0, CA / 3.0, CZ / 3.0)
    amplitude = 1.0 / math.sqrt(width[1] * width[2] / width[0])

    cell = iota((24, SLOTS), 0).astype(F32) - GHOST
    d = cell + back[0] * CR
    profile, slope = shape_pair(d - centre[0], (d >= 0.0) & (d < span[0] * CR), width[0])
    arc = step * (0.5 * (CR * N_RAD) + (r * CR).astype(F32) + cell + 0.5)
    shape_r[0] = arc * slope
    shape_r[1] = profile
    shape_r[2] = arc * profile

    d = iota((ROWS, SLOTS), 0).astype(F32) - FIRST + back[1] * CA
    d = jnp.where(d < 0.0, d + CA * N_ANG, d)
    d = jnp.where(d >= CA * N_ANG, d - CA * N_ANG, d)
    ang_profile, ang_slope = shape_pair(d - centre[1], d < span[1] * CA, width[1])

    d = iota((2 * CZ, SLOTS), 0).astype(F32) + back[2] * CZ
    d = jnp.where(d >= CZ * N_AX, d - CZ * N_AX, d)
    ax_profile, ax_slope = shape_pair(d - centre[2], d < span[2] * CZ, width[2])
    ax_high, ax_low = split2(jnp.concatenate([ax_profile, ax_slope], axis=1))
    ax_factors = jnp.concatenate([ax_high, ax_high, ax_low], axis=0)


    sums = [jnp.zeros((8, SLOTS), F32) for _ in range(3)]

    def project(first_plane, per):
        block = jnp.concatenate(
            [ref[pl.ds(1 + first_plane, per), window].reshape(per * ROWS, CZ) for ref in (own, other)],
            axis=1,
        )
        high, low = split2(block)
        projected = jnp.dot(
            jnp.concatenate([high, low, high], axis=1), ax_factors, preferred_element_type=F32
        )
        for p in range(per):
            along = [jnp.zeros((8, SLOTS), F32)] * 3
            for t in range(ROWS // 8):
                top = p * ROWS + 8 * t
                plain, sloped = projected[top : top + 8, :SLOTS], projected[top : top + 8, SLOTS:]
                ang_p, ang_s = ang_profile[8 * t : 8 * t + 8], ang_slope[8 * t : 8 * t + 8]
                along = [along[0] + plain * ang_p, along[1] + plain * ang_s, along[2] + sloped * ang_p]
            for k in range(3):
                row = first_plane + p
                sums[k] = sums[k] + shape_r[k, row : row + 1, :] * along[k]

    project(0, 11)
    project(11, 11)

    strength = charge * amplitude
    force = [jnp.sum(s, axis=0, keepdims=True) * strength for s in sums]

    target, low = entry(18), entry(19)
    to = jnp.where(iota((32, SLOTS), 0).astype(F32) == target, 1.0, 0.0).astype(BF16)
    here = iota((64, SLOTS), 0).astype(F32) == low
    spread = jnp.concatenate([jnp.where(here, f, 0.0) for f in force] + [jnp.zeros((64, SLOTS), F32)], axis=0)
    placed = jnp.zeros((32, 256), F32)
    for piece in split2(spread):
        placed = placed + nt(to, piece)
    for k in range(32):
        part[k] = placed[k : k + 1, :]

    pl.semaphore_wait(barrier, len(targets) + odd * len(far_column))

    @pl.when(odd == 1)
    def _():
        for target in far_column:
            pl.semaphore_signal(ready, inc=1, device_id=target, device_id_type=MESH)


    def send(source, landing, number, device):
        copy = pltpu.make_async_remote_copy(
            src_ref=source,
            dst_ref=landing,
            send_sem=sems.at[0, number],
            recv_sem=sems.at[1, number],
            device_id=device,
            device_id_type=MESH,
        )
        copy.start()
        return copy

    def wait(ref, side, number):
        pltpu.make_async_copy(ref, ref, sems.at[side, number]).wait()

    for slot, device, place in plane:
        send(part.at[place], plane_in.at[slot - 1], 1, device)
    rows = pl.ds(8, CA)
    far = [
        send(own.at[22, rows], rad_in.at[0, 2], 2, around[0]),
        send(own.at[1, rows], rad_in.at[1, 0], 3, around[1]),
    ]
    partner = (r, a, 1 - x)
    below, above, inner = pl.ds(2, 2), pl.ds(20, 2), pl.ds(4, CR)
    ax_copies = [
        send(other.at[planes], ax_in.at[planes], number, partner)
        for planes, number in ((above, 0), (below, 11), (inner, 12))
    ]

    def join(p):
        full[p] = own[p, 8:56] + ax_in[p, 8:56]
        edge[0, p] = own[p, 56:60] + ax_in[p, 56:60]
        edge[1, p] = own[p, 4:8] + ax_in[p, 4:8]

    ax_copies[0].wait_recv()
    join(20)
    join(21)
    near = [send(full.at[above], rad_in.at[0, pl.ds(0, 2)], 13, around[0])]
    ax_copies[1].wait_recv()
    join(2)
    join(3)
    near.append(send(full.at[below], rad_in.at[1, pl.ds(1, 2)], 14, around[1]))
    copies = [
        send(edge.at[0, above], corner_in.at[0], 6, around[4]),
        send(edge.at[0, below], corner_in.at[1], 7, around[5]),
        send(edge.at[1, above], corner_in.at[2], 8, around[6]),
        send(edge.at[1, below], corner_in.at[3], 9, around[7]),
    ]
    ax_copies[2].wait_recv()
    for p in range(4, 4 + CR):
        join(p)
    copies.append(send(edge.at[0, inner], ang_in.at[0], 4, around[2]))
    copies.append(send(edge.at[1, inner], ang_in.at[1], 5, around[3]))
    out_ref[...] = full[inner]

    wait(plane_in, 1, 1)
    me_place = (r // 2) * 8 + lax.rem(a, 8)
    mine[...] = part[me_place] + jnp.sum(plane_in[...], axis=0)

    def pass_on(far):
        for slot, device in column:
            if (slot >= 8) == far:
                send(mine, column_in.at[slot - 1], 10, device)

    @pl.when(odd == 1)
    def _():
        pass_on(True)

    pass_on(False)

    @pl.when(odd == 0)
    def _():
        pl.semaphore_wait(ready, len(far_column))
        pass_on(True)

    for copy in copies:
        copy.wait()
    out_ref[:, 0:4, :] = out_ref[:, 0:4, :] + ang_in[0]
    out_ref[:, CA - 4 : CA, :] = out_ref[:, CA - 4 : CA, :] + ang_in[1]
    for k in range(4):
        planes = pl.ds(14 * (k % 2), 2)
        rows = pl.ds((CA - 4) * (k // 2), 4)
        out_ref[planes, rows, :] = out_ref[planes, rows, :] + corner_in[k]
    for copy in far + near:
        copy.wait()
    out_ref[0:3] = out_ref[0:3] + rad_in[0]
    out_ref[13:16] = out_ref[13:16] + rad_in[1]
    for copy in ax_copies:
        copy.wait_send()

    wait(column_in, 1, 10)
    total = mine[...] + jnp.sum(column_in[...], axis=0)
    me_column = (lax.rem(r, 2) * 4 + a // 8) * 2 + x
    for k in range(3):
        turned = pltpu.roll(jnp.broadcast_to(total, (8, 256)), lax.rem(512 - 64 * k - 4 * me_column, 256), 1)
        force_ref[k : k + 1, :] = turned[0:1, 0:4]
    wait(plane_in, 0, 1)
    wait(column_in, 0, 10)


def store(potential_ref, force_ref, potential_out, force_out, sems):
    copies = [
        pltpu.make_async_copy(potential_ref, potential_out, sems.at[0]),
        pltpu.make_async_copy(force_ref, force_out, sems.at[1]),
    ]
    for copy in copies:
        copy.start()
    for copy in copies:
        copy.wait()


def shards(start_potential, charge_density, box_anchor, box_extent, atom_center, atom_charge, atom_place):
    whole = pl.BlockSpec(memory_space=pltpu.VMEM)
    operands = [start_potential, charge_density, box_anchor, box_extent, atom_center]
    operands += [atom_charge.reshape(1, ATOMS), atom_place.reshape(1, ATOMS)]
    grid = (PLANES + 2, CA + 16, CZ)
    potential, forces = pl.pallas_call(
        kernel,
        out_shape=(
            jax.ShapeDtypeStruct((CR, CA, CZ), F32),
            jax.ShapeDtypeStruct((3, 4), F32),
        ),
        in_specs=[pl.BlockSpec(memory_space=pltpu.HBM)] * 7,
        out_specs=(whole, whole),
        scratch_shapes=[
            *[pltpu.VMEM(grid, F32)] * 5,
            pltpu.VMEM((4, 24, CZ), F32),
            pltpu.VMEM((3, 24, SLOTS), F32),
            pltpu.VMEM(grid, F32),
            pltpu.VMEM((PLANES + 2, CA, CZ), F32),
            pltpu.VMEM((2, PLANES + 2, 4, CZ), F32),
            pltpu.VMEM((2, GHOST, CA, CZ), F32),
            pltpu.VMEM((2, CR, 4, CZ), F32),
            pltpu.VMEM((4, 2, 4, CZ), F32),
            pltpu.VMEM((32, 1, 256), F32),
            pltpu.VMEM((31, 1, 256), F32),
            pltpu.VMEM((1, 256), F32),
            pltpu.VMEM((15, 1, 256), F32),
            pltpu.VMEM((3, ATOMS), jnp.int32),
            pltpu.VMEM((3, ATOMS), jnp.int32),
            pltpu.VMEM((3, ATOMS), F32),
            pltpu.VMEM((1, ATOMS), F32),
            pltpu.VMEM((1, ATOMS), jnp.int32),
            pltpu.SemaphoreType.REGULAR,
            pltpu.SemaphoreType.DMA((2, 15)),
            pltpu.SemaphoreType.DMA((7,)),
        ],
        compiler_params=pltpu.CompilerParams(
            collective_id=0, has_side_effects=True, vmem_limit_bytes=40 * 1024 * 1024
        ),
    )(*[pltpu.with_memory_space_constraint(v, pltpu.HBM) for v in operands])
    hbm = pl.BlockSpec(memory_space=pltpu.HBM)
    return pl.pallas_call(
        store,
        out_shape=(
            jax.ShapeDtypeStruct((CR, CA, CZ), F32),
            jax.ShapeDtypeStruct((3, 4), F32),
        ),
        in_specs=[whole] * 2,
        out_specs=(hbm, hbm),
        scratch_shapes=[pltpu.SemaphoreType.DMA((2,))],
    )(*[pltpu.with_memory_space_constraint(v, pltpu.VMEM) for v in (potential, forces)])


def solution(mesh):
    placed = (P("rad", "ang", "ax"), P("rad", "ang", "ax"), P(), P(), P(), P(), P())
    return jax.shard_map(
        shards,
        mesh=mesh,
        in_specs=placed,
        out_specs=(P("rad", "ang", "ax"), P(None, ("rad", "ang", "ax"))),
        check_vma=False,
    )
```
